32 devices in a mesh: rows: 8 (over z, y), dims: 4 (over x, core).
Axes of the slice: x: 2, y: 2, z: 4, core: 2. Of those that a mesh axis runs over, the one named last changes fastest.
Arguments:
- table: bfloat16 [1, 256, 32768], P(None, 'dims', 'rows'), may hold values from -6 to 6
- accum: float32 [1, 32768], P(None, 'rows'), may hold values from 0.5 to 8
- grad_pooled: bfloat16 [1, 256, 1024], P(None, 'dims', 'rows'), may hold values from -6 to 6
- sample_slot: int32 [1, 8, 8, 1280], P(None, 'rows'), may hold values from 0 to 127
- row_slot: int32 [1, 8, 8, 1280], P(None, 'rows'), may hold values from 0 to 4095
- weight: int32 [1, 8, 8, 1280], P(None, 'rows'), may hold values from 1 to 3
- send_count: int32 [1, 8, 8], P(None, 'rows'), may hold values from 1 to 1280, as said below
Outputs:
- pooled: float32 [1, 256, 1024], P(None, 'dims', 'rows')
- new_table: bfloat16 [1, 256, 32768], P(None, 'dims', 'rows')
- new_accum: float32 [1, 32768], P(None, 'rows')
The draws below stay inside these ranges and needn't reach their ends.
Inputs may be any that keep to these rules, and one draw needn't show every extreme that they name: `send_count`: at most 1280 live entries from one row shard to one owner per feature; in every feature one owner receives exactly 1280 from every row shard. Slots at or after the count are unused.
All inputs are finite; a program needn't handle non-finite values.
Results may differ from the reference program's by a relative error of at most 0.001.
Values may be sent and summed in bfloat16 or wider, within the bound.
No kernel may reach another device: no remote copies, remote signals or barrier semaphores. Data moves between devices by JAX's collectives and lax.ppermute only.
A program may use at most 64 MiB of HBM per device.

```python
import math
import jax
import jax.numpy as jnp
import numpy as np
from jax import lax

D = 256
FEAT = 1
LR = 4096
SPD = 128
CAP = 1280
ROWS = 32768
SAMPLES = 1024
N_ROWS = 8


def draw_send_count(key, part):
    base_key, full_key = jax.random.split(jax.random.fold_in(key, 17))
    base_count = jax.random.randint(base_key, (FEAT, N_ROWS, N_ROWS), 1, CAP + 1)
    full_owner = jax.random.randint(full_key, (FEAT, 1, 1), 0, N_ROWS)
    owner_index = lax.broadcasted_iota(jnp.int32, (FEAT, N_ROWS, N_ROWS), 2)
    return jnp.where(owner_index == full_owner, CAP, base_count).astype(jnp.int32)


def plant(drawn, own_key, least, high):
    dims = drawn.shape
    place = [jax.random.randint(jax.random.fold_in(own_key, axis), (), 0, dims[axis]) for axis in range(len(dims))]
    drawn = drawn.at[tuple(place)].set(least)
    longest = dims.index(max(dims))
    place[longest] = (place[longest] + 1) % dims[longest]
    return drawn.at[tuple(place)].set(high)


def level_of(key, shape, shards, least, largest):
    def one(position, parts):
        heights = jax.random.uniform(jax.random.fold_in(jax.random.fold_in(key, 6), position), (parts,), jnp.float32, least / len(shards), largest / len(shards))
        return jnp.repeat(jnp.exp(heights), shape[position] // parts).reshape((-1,) + (1,) * (len(shape) - position - 1))

    loudness = one(*shards[0])
    for cut in shards[1:]:
        loudness = loudness * one(*cut)
    return loudness


def rank_table(number_of, slope):
    loads = [(1 << 20) // math.isqrt(standing ** slope) + 1 for standing in range(1, number_of + 1)]
    spread = 1 + sum(loads) // (1 << 30)
    return np.cumsum(np.array([max(1, weight // spread) for weight in loads]))


def ranked_ids(rng, shape, amount, skew):
    table = rank_table(amount, skew)
    ticket = jax.random.randint(jax.random.fold_in(rng, 1), shape, 0, int(table[amount - 1]))
    rank = jnp.searchsorted(jnp.asarray(table, jnp.int32), ticket, side="right")
    return jax.random.permutation(jax.random.fold_in(rng, 2), amount)[rank].astype(jnp.int32)


def centred(rng, dims, width, reach, cuts=(), kind=jnp.bfloat16):
    entries = jax.random.normal(rng, dims, jnp.float32) * width
    if len(cuts) > 0:
        entries = level_of(rng, dims, cuts, -0.22, 0.18) * entries
    return jnp.clip(entries, min=-reach, max=reach).astype(kind)


def setup_inputs(seed: int = 0) -> dict:
    key_list = jax.random.split(jax.random.key(seed), 8)
    return {
        "table": centred(key_list[0], (FEAT, D, ROWS), 1.0, 6.0, ((1, 4), (2, 8))),
        "accum": jnp.clip(jnp.exp(math.log(8.0) - 2.7725887 * jax.random.uniform(key_list[1], (FEAT, ROWS), jnp.float32) ** level_of(key_list[1], (FEAT, ROWS), ((1, 8),), -0.2, 0.2)), 0.5, 8.0),
        "grad_pooled": centred(key_list[2], (FEAT, D, SAMPLES), 1.0, 6.0, ((1, 4), (2, 8))),
        "sample_slot": plant(jax.random.randint(key_list[3], (FEAT, N_ROWS, N_ROWS, CAP), 0, SPD), jax.random.fold_in(key_list[3], 1), 0, SPD - 1).astype(jnp.int32),
        "row_slot": plant(ranked_ids(key_list[4], (FEAT, N_ROWS, N_ROWS, CAP), LR, 2), jax.random.fold_in(key_list[4], 3), 0, LR - 1).astype(jnp.int32),
        "weight": plant(jax.random.randint(key_list[5], (FEAT, N_ROWS, N_ROWS, CAP), 1, 4), jax.random.fold_in(key_list[5], 1), 1, 3).astype(jnp.int32),
        "send_count": draw_send_count(jax.random.fold_in(key_list[7], 71), 0),
    }


step_size = 0.3

def reference(table, accum, grad_pooled, sample_slot, row_slot, weight, send_count):
    feat_count = table.shape[0]
    peer_count = send_count.shape[1]
    slot_count = sample_slot.shape[3]
    own_samples = grad_pooled.shape[2] // peer_count
    row_local = table.shape[2] // peer_count
    slot_index = lax.broadcasted_iota(jnp.int32, sample_slot.shape, 3)
    live_mask = slot_index < send_count[..., None]
    live_weights = jnp.where(live_mask, weight, 0).astype(jnp.float32)
    source = lax.broadcasted_iota(jnp.int32, sample_slot.shape, 1)
    owner_index = lax.broadcasted_iota(jnp.int32, sample_slot.shape, 2)
    global_row = (source * row_local + row_slot).astype(jnp.int32)
    target = (owner_index * own_samples + sample_slot).astype(jnp.int32)
    pooled_list = []
    table_list = []
    accum_list = []
    for feature in range(feat_count):
        table_rows = table[feature].astype(jnp.float32)
        grad_rows = grad_pooled[feature].astype(jnp.float32)

        def accumulate(state_pair, entry_group):
            pooled, row_grad = state_pair
            row_index, target_index, weight_row = entry_group
            row_index = row_index.reshape(-1)
            target_index = target_index.reshape(-1)
            weight_row = weight_row.reshape(-1)
            pooled = pooled.at[:, target_index].add(table_rows[:, row_index] * weight_row[None, :])
            row_grad = row_grad.at[:, row_index].add(grad_rows[:, target_index] * weight_row[None, :])
            return ((pooled, row_grad), None)
        start_state = (jnp.zeros((D, peer_count * own_samples), jnp.float32), jnp.zeros((D, peer_count * row_local), jnp.float32))
        (pooled, row_grad), _ = lax.scan(accumulate, start_state, (global_row[feature], target[feature], live_weights[feature]))
        new_accum = accum[feature] + lax.optimization_barrier(jnp.sum(row_grad * row_grad, axis=0)) / D
        new_rows = (table_rows - step_size * row_grad / jnp.sqrt(new_accum)[None, :]).astype(jnp.bfloat16)
        pooled_list.append(pooled)
        table_list.append(new_rows)
        accum_list.append(new_accum)
    return (jnp.stack(pooled_list), jnp.stack(table_list), jnp.stack(accum_list))
```

```python
import functools
import math

import jax
import jax.numpy as jnp
from jax import lax
from jax.experimental import pallas as pl
from jax.experimental.pallas import tpu as pltpu
from jax.sharding import PartitionSpec as P

D = 256


step_size = 0.3


LANES = 128
CHUNK = 256
NARROW = jnp.float8_e4m3fn
EXACT = 256.0
FAST_BYTES = 24 << 20


def factor_product(row, sample, weight, count, low, span, depth):
    row = row[:, :depth]
    slot = lax.broadcasted_iota(jnp.int32, row.shape, 1)
    live = jnp.where(slot < count, weight[:, :depth], 0).astype(jnp.bfloat16)
    left_key = (row % low).astype(jnp.int16)
    right_key = ((row // low) * LANES + sample[:, :depth]).astype(jnp.int16)
    left_iota = lax.broadcasted_iota(jnp.int16, (low, depth), 0)
    right_iota = lax.broadcasted_iota(jnp.int16, (span * LANES, depth), 0)
    zero = jnp.bfloat16(0)
    left = jnp.where(left_iota == left_key, live, zero).astype(NARROW)
    right = jnp.where(right_iota == right_key, jnp.bfloat16(1), zero).astype(NARROW)
    return lax.dot_general(
        left, right, (((1,), (1,)), ((), ())), preferred_element_type=jnp.float32
    )


def count_kernel(
    owner_ref, count_ref, row_ref, sample_ref, weight_ref, table_ref,
    counts_ref, pooled_ref, low_ref, flag_ref, peak_ref, spill_ref, sem,
    *, low, span, group, chunks,
):
    step = pl.program_id(0)

    @pl.when(step == 0)
    def _():
        peak_ref[...] = jnp.zeros_like(peak_ref)

    for member in range(group):
        owner = owner_ref[step * group + member]
        count = count_ref[owner]
        row = row_ref[pl.ds(owner, 1), :]
        sample = sample_ref[pl.ds(owner, 1), :]
        weight = weight_ref[pl.ds(owner, 1), :]
        needed = jnp.maximum((count + CHUNK - 1) // CHUNK, 1)
        for chunk in range(1, chunks + 1):

            @pl.when(needed == chunk)
            def _(chunk=chunk):
                depth = min(chunk * CHUNK, row.shape[1])
                counts = factor_product(row, sample, weight, count, low, span, depth)
                counts = counts.astype(jnp.bfloat16)
                peak = peak_ref[...]
                for part in range(span):
                    piece = counts[:, part * LANES : (part + 1) * LANES]
                    counts_ref[
                        0, part * low : (part + 1) * low, member * LANES : (member + 1) * LANES
                    ] = piece
                    peak = jnp.maximum(peak, piece)
                peak_ref[...] = peak

    pooled = jnp.dot(table_ref[...], counts_ref[0], preferred_element_type=jnp.float32)
    for member in range(group):
        pooled_ref[step * group + member] = pooled[:, member * LANES : (member + 1) * LANES]

    @pl.when(step == pl.num_programs(0) - 1)
    def _():
        large = jnp.max(peak_ref[...].astype(jnp.float32)) >= EXACT
        flag_ref[0] = large.astype(jnp.int32)

        @pl.when(large)
        def _():
            def redo(index, carry):
                owner = owner_ref[index]
                counts = factor_product(
                    row_ref[pl.ds(owner, 1), :], sample_ref[pl.ds(owner, 1), :],
                    weight_ref[pl.ds(owner, 1), :], count_ref[owner], low, span,
                    row_ref.shape[1],
                )
                rest = (counts - counts.astype(jnp.bfloat16).astype(jnp.float32)).astype(
                    jnp.bfloat16
                )
                for part in range(span):
                    spill_ref[part * low : (part + 1) * low, :] = rest[
                        :, part * LANES : (part + 1) * LANES
                    ]
                pooled_ref[index] += jnp.dot(
                    table_ref[...], spill_ref[...], preferred_element_type=jnp.float32
                )
                copy = pltpu.make_async_copy(spill_ref, low_ref.at[index], sem)
                copy.start()
                copy.wait()
                return carry

            lax.fori_loop(0, owner_ref.shape[0], redo, 0)


def count_call(owners, send_count, row, sample, weight, table, own_samples):
    total = owners.shape[0]
    dim_local, row_local = table.shape
    slots = row.shape[1]
    low = math.gcd(row_local, 512)
    span = row_local // low
    group = 2 if total % 2 == 0 else 1
    whole = lambda shape: pl.BlockSpec(shape, lambda step, *_: (0,) * len(shape))
    return pl.pallas_call(
        functools.partial(
            count_kernel, low=low, span=span, group=group, chunks=-(-slots // CHUNK)
        ),
        grid_spec=pltpu.PrefetchScalarGridSpec(
            num_scalar_prefetch=2,
            grid=(total // group,),
            in_specs=[whole(row.shape)] * 3 + [whole(table.shape)],
            out_specs=[
                pl.BlockSpec((1, row_local, group * LANES), lambda step, *_: (step, 0, 0)),
                whole((total, dim_local, LANES)),
                pl.BlockSpec(memory_space=pl.ANY),
                pl.BlockSpec(memory_space=pltpu.SMEM),
            ],
            scratch_shapes=[
                pltpu.VMEM((low, LANES), jnp.bfloat16),
                pltpu.VMEM((row_local, LANES), jnp.bfloat16),
                pltpu.SemaphoreType.DMA,
            ],
        ),
        out_shape=[
            jax.ShapeDtypeStruct((total // group, row_local, group * LANES), jnp.bfloat16),
            jax.ShapeDtypeStruct((total, dim_local, LANES), jnp.float32),
            jax.ShapeDtypeStruct((total, row_local, LANES), jnp.bfloat16),
            jax.ShapeDtypeStruct((1,), jnp.int32),
        ],
        compiler_params=pltpu.CompilerParams(vmem_limit_bytes=24 << 20),
        name="counts",
    )(owners, send_count, row, sample, weight, table)


def grad_kernel(*refs, parts, groups, places, block):
    flag_refs = refs[:parts]
    counts_refs = refs[parts : 2 * parts]
    low_refs = refs[2 * parts : 3 * parts]
    grads = refs[3 * parts : -4]
    grad_ref, square_ref, spill_ref, sem = refs[-4:]
    start = pl.program_id(0) * block
    total = None
    base = 0
    for part in range(parts):
        pairs = counts_refs[part].shape[0]
        for pair in range(pairs):
            columns = []
            for member in range(groups[part]):
                source, column = places[base + pair * groups[part] + member]
                columns.append(grads[source][:, column * LANES : (column + 1) * LANES])
            left = jnp.concatenate(columns, axis=1)
            term = lax.dot_general(
                left, counts_refs[part][pair], (((1,), (1,)), ((), ())),
                preferred_element_type=jnp.float32,
            )
            total = term if total is None else total + term
        base += pairs * groups[part]
    grad_ref[...] = total

    base = 0
    for part in range(parts):
        owners = counts_refs[part].shape[0] * groups[part]

        @pl.when(flag_refs[part][0] > 0)
        def _(part=part, base=base, owners=owners):
            for index in range(owners):
                source, column = places[base + index]
                copy = pltpu.make_async_copy(
                    low_refs[part].at[index, pl.ds(start, block)], spill_ref, sem
                )
                copy.start()
                copy.wait()
                grad_ref[...] += lax.dot_general(
                    grads[source][:, column * LANES : (column + 1) * LANES], spill_ref[...],
                    (((1,), (1,)), ((), ())), preferred_element_type=jnp.float32,
                )

        base += owners
    final = grad_ref[...]
    square_ref[...] = jnp.sum(final * final, axis=0, keepdims=True)


def grad_call(flags, counts, lows, grads, places):
    parts = len(counts)
    row_local = counts[0].shape[1]
    dim_local = grads[0].shape[0]
    groups = [c.shape[2] // LANES for c in counts]
    block = math.gcd(row_local, 1024)
    return pl.pallas_call(
        functools.partial(
            grad_kernel, parts=parts, groups=groups, places=places, block=block
        ),
        grid=(row_local // block,),
        in_specs=[pl.BlockSpec(memory_space=pltpu.SMEM)] * parts
        + [pl.BlockSpec((c.shape[0], block, c.shape[2]), lambda step: (0, step, 0)) for c in counts]
        + [pl.BlockSpec(memory_space=pl.ANY)] * parts
        + [pl.BlockSpec(g.shape, lambda step: (0, 0)) for g in grads],
        out_specs=[
            pl.BlockSpec((dim_local, block), lambda step: (0, step)),
            pl.BlockSpec((1, block), lambda step: (0, step)),
        ],
        out_shape=[
            jax.ShapeDtypeStruct((dim_local, row_local), jnp.float32),
            jax.ShapeDtypeStruct((1, row_local), jnp.float32),
        ],
        scratch_shapes=[pltpu.VMEM((block, LANES), jnp.bfloat16), pltpu.SemaphoreType.DMA],
        compiler_params=pltpu.CompilerParams(vmem_limit_bytes=24 << 20),
        name="grads",
    )(*flags, *counts, *lows, *grads)


def flip(value, axis, mask):
    size = lax.axis_size(axis)
    return lax.ppermute(value, axis, [(index, index ^ mask) for index in range(size)])


def staged(table, accum, grad_pooled, sample, row, weight, send_count):
    peers = lax.axis_size("rows")
    own_samples = grad_pooled.shape[1]
    me = lax.axis_index("rows")
    bits = [1 << place for place in range(peers.bit_length() - 1)]
    gather_bits = bits[-1:] + bits[:-1]
    reduce_bits = bits[:-1] + bits[-1:]
    stages = len(bits)
    masks = [None] * stages
    phases = [None] * stages
    masks[-1] = [0]
    for stage in reversed(range(stages)):
        if stage < stages - 1:
            masks[stage] = phases[stage + 1] + masks[stage + 1]
        phases[stage] = [reduce_bits[stage] ^ mask for mask in masks[stage]]
    phases[-1] = phases[-1] + [0]

    pieces = [grad_pooled]
    where = [0]
    flags, counts, lows = [], [], []
    received = []
    sent_grad = flip(grad_pooled, "rows", gather_bits[0])
    own = None
    for stage in range(stages):
        owners = me ^ jnp.asarray(phases[stage], jnp.int32)
        found, partial, low, flag = count_call(
            owners, send_count, row, sample, weight, table, own_samples
        )
        partial, sent_grad = lax.optimization_barrier((partial, sent_grad))
        flags.append(flag)
        counts.append(found)
        lows.append(low)
        pieces.append(sent_grad)
        where = where + [mask ^ gather_bits[stage] for mask in where]
        offset = 0
        for earlier in range(stage):
            begin = len(masks[earlier]) - len(masks[stage]) - len(phases[stage]) + (stage == stages - 1)
            take = received[earlier][begin : begin + len(phases[stage])]
            partial = partial + take
        if stage == stages - 1:
            own = partial[1]
            partial = partial[:1]
        received.append(flip(partial, "rows", reduce_bits[stage]))
        if stage < stages - 1:
            sent_grad = flip(jnp.concatenate(pieces, axis=1), "rows", gather_bits[stage + 1])
    spots = {}
    position = 0
    for index, piece in enumerate(pieces):
        for column in range(piece.shape[1] // own_samples):
            spots[where[position]] = (index, column)
            position += 1
    places = [spots[mask] for phase in phases for mask in phase]
    row_grad, square = grad_call(flags, counts, lows, pieces, places)
    pooled = own + received[-1][0]

    return pooled, row_grad, square


def share(square):
    size = lax.axis_size("dims")
    terms = [square]
    far = size // 2
    order = []
    while far >= 1:
        order.append(far)
        far //= 2
    for mask in order:
        terms = terms + [flip(term, "dims", mask) for term in terms]
    while len(terms) > 1:
        half = len(terms) // 2
        terms = [terms[index] + terms[index + half] for index in range(half)]
    return terms[0]


def update(table, accum, row_grad, square):
    new_accum = accum[None, :] + share(square) / D
    scale = step_size / jnp.sqrt(new_accum)
    new_table = (table.astype(jnp.float32) - row_grad * scale).astype(jnp.bfloat16)
    return new_table, new_accum[0]


def fits(table, grad_pooled, peers):
    return (
        peers & (peers - 1) == 0
        and peers > 1
        and grad_pooled.shape[2] == LANES
        and peers * table.shape[2] * LANES * 2 <= FAST_BYTES
    )


def shards(table, accum, grad_pooled, sample_slot, row_slot, weight, send_count):
    peers = lax.axis_size("rows")
    if not fits(table, grad_pooled, peers):
        return plain(table, accum, grad_pooled, sample_slot, row_slot, weight, send_count)
    outs = []
    for feature in range(table.shape[0]):
        pooled, row_grad, square = staged(
            table[feature], accum[feature], grad_pooled[feature], sample_slot[feature, 0],
            row_slot[feature, 0], weight[feature, 0], send_count[feature, 0],
        )
        new_table, new_accum = update(table[feature], accum[feature], row_grad, square)
        outs.append((pooled, new_table, new_accum))
    return tuple(jnp.stack(out) for out in zip(*outs))


def plain(table, accum, grad_pooled, sample_slot, row_slot, weight, send_count):
    feat_count, dim_local, row_local = table.shape
    peer_count = lax.axis_size("rows")
    own_samples = grad_pooled.shape[2]
    slot_count = sample_slot.shape[3]
    entry_count = peer_count * slot_count
    block_rows = math.gcd(row_local, 512)
    block_count = row_local // block_rows
    sample_local = sample_slot.reshape(feat_count, peer_count, slot_count)
    row_index = row_slot.reshape(feat_count, peer_count, slot_count)
    flat_rows = row_index.reshape(feat_count, 1, entry_count)
    live_count = send_count.reshape(feat_count, peer_count)
    slot_iota = lax.broadcasted_iota(jnp.int32, (1, 1, slot_count), 2)
    live_mask = slot_iota < live_count[:, :, None]
    weights = jnp.where(live_mask, weight.reshape(feat_count, peer_count, slot_count), 0)
    flat_weights = weights.reshape(feat_count, 1, entry_count).astype(jnp.bfloat16)
    block_iota = lax.broadcasted_iota(jnp.int32, (1, block_rows, 1), 1)

    def lookup_block(carry, block):
        start = block * block_rows
        table_part = lax.dynamic_slice_in_dim(table, start, block_rows, 2)
        selector = (flat_rows == block_iota + start).astype(jnp.bfloat16)
        return (
            carry
            + jnp.einsum("fdr,fre->fde", table_part, selector, preferred_element_type=jnp.float32),
            None,
        )

    looked_up, _ = lax.scan(
        lookup_block,
        jnp.zeros((feat_count, dim_local, entry_count), jnp.float32),
        jnp.arange(block_count, dtype=jnp.int32),
    )
    picked = looked_up.astype(jnp.bfloat16).reshape(feat_count, dim_local, peer_count, slot_count)
    positions = lax.broadcasted_iota(jnp.int32, (1, 1, 1, own_samples), 3)
    onehot = jnp.where(sample_local[..., None] == positions, weights[..., None], 0).astype(
        jnp.bfloat16
    )
    pooled = lax.psum_scatter(
        jnp.einsum("fdnk,fnkj->nfdj", picked, onehot, preferred_element_type=jnp.float32),
        "rows",
        scatter_dimension=0,
        tiled=True,
    ).reshape(feat_count, dim_local, own_samples)
    all_grads = lax.all_gather(grad_pooled, "rows", axis=2, tiled=True)
    all_grads = all_grads.reshape(feat_count, dim_local, peer_count, own_samples)
    selector = (sample_local[..., None] == positions).astype(jnp.bfloat16)
    entry_values = jnp.einsum(
        "fdnj,fnkj->fdnk", all_grads, selector, preferred_element_type=jnp.float32
    ).astype(jnp.bfloat16)
    entry_flat = entry_values.reshape(feat_count, dim_local, entry_count)

    def gradient_block(block):
        start = block * block_rows
        weighted = jnp.where(flat_rows == block_iota + start, flat_weights, 0)
        return jnp.einsum("fde,fre->fdr", entry_flat, weighted, preferred_element_type=jnp.float32)

    grad_blocks = lax.map(gradient_block, jnp.arange(block_count, dtype=jnp.int32))
    row_grad = jnp.moveaxis(grad_blocks, 0, 2).reshape(feat_count, dim_local, row_local)
    squares = jnp.sum(row_grad * row_grad, axis=1)
    norm_total = lax.psum(squares, "dims")
    new_accum = accum + norm_total / D
    new_table = (
        table.astype(jnp.float32) - step_size * row_grad / jnp.sqrt(new_accum)[:, None, :]
    ).astype(jnp.bfloat16)
    return (pooled, new_table, new_accum)


def solution(mesh):
    return jax.shard_map(
        shards,
        mesh=mesh,
        in_specs=(
            P(None, "dims", "rows"),
            P(None, "rows"),
            P(None, "dims", "rows"),
            P(None, "rows", None, None),
            P(None, "rows", None, None),
            P(None, "rows", None, None),
            P(None, "rows", None),
        ),
        out_specs=(P(None, "dims", "rows"), P(None, "dims", "rows"), P(None, "rows")),
        check_vma=False,
    )
```

```python
import functools
import math

import jax
import jax.numpy as jnp
from jax import lax
from jax.experimental import pallas as pl
from jax.experimental.pallas import tpu as pltpu
from jax.sharding import PartitionSpec as P


D = 256


step_size = 0.3


LANES = 128
CHUNK = 256
NARROW = jnp.float8_e4m3fn
EXACT = 256.0
FAST_BYTES = 24 << 20
VMEM_LIMIT = 16 << 20


def factor_product(row, sample, weight, count, low, span, depth):
    row = row[:, :depth]
    slot = lax.broadcasted_iota(jnp.int32, row.shape, 1)
    live = jnp.where(slot < count, weight[:, :depth], 0).astype(jnp.bfloat16)
    left_key = (row % low).astype(jnp.int16)
    right_key = ((row // low) * LANES + sample[:, :depth]).astype(jnp.int16)
    left_iota = lax.broadcasted_iota(jnp.int16, (low, depth), 0)
    right_iota = lax.broadcasted_iota(jnp.int16, (span * LANES, depth), 0)
    zero = jnp.bfloat16(0)
    left = jnp.where(left_iota == left_key, live, zero).astype(NARROW)
    right = jnp.where(right_iota == right_key, jnp.bfloat16(1), zero).astype(NARROW)
    return lax.dot_general(
        left, right, (((1,), (1,)), ((), ())), preferred_element_type=jnp.float32
    )


def count_kernel(
    count_hbm, row_hbm, sample_hbm, weight_hbm, table_hbm,
    counts_ref, pooled_ref, low_ref, flag_ref,
    count_ref, row_ref, sample_ref, weight_ref, table_ref, peak_ref, spill_ref, sems,
    *, masks, low, span, chunks,
):
    loads = [
        pltpu.make_async_copy(source, target, sems.at[index])
        for index, (source, target) in enumerate(
            (
                (count_hbm, count_ref),
                (row_hbm, row_ref),
                (sample_hbm, sample_ref),
                (weight_hbm, weight_ref),
                (table_hbm, table_ref),
            )
        )
    ]
    for load in loads:
        load.start()
    me = lax.axis_index("rows")
    peak_ref[...] = jnp.zeros_like(peak_ref)
    for load in loads[:-1]:
        load.wait()

    def owner_of(index):
        owner = me ^ masks[0]
        for place, mask in enumerate(masks[1:], 1):
            owner = jnp.where(index == place, me ^ mask, owner)
        return owner

    def count_pair(pair, carry):
        for member in range(2):
            owner = owner_of(2 * pair + member)
            count = count_ref[0, owner]
            row = row_ref[pl.ds(owner, 1), :]
            sample = sample_ref[pl.ds(owner, 1), :]
            weight = weight_ref[pl.ds(owner, 1), :]
            needed = jnp.maximum((count + CHUNK - 1) // CHUNK, 1)
            for chunk in range(1, chunks + 1):

                @pl.when(needed == chunk)
                def _(chunk=chunk):
                    depth = min(chunk * CHUNK, row.shape[1])
                    counts = factor_product(row, sample, weight, count, low, span, depth)
                    counts = counts.astype(jnp.bfloat16)
                    peak = peak_ref[...]
                    for part in range(span):
                        piece = counts[:, part * LANES : (part + 1) * LANES]
                        counts_ref[
                            pair, part * low : (part + 1) * low,
                            member * LANES : (member + 1) * LANES,
                        ] = piece
                        peak = jnp.maximum(peak, piece)
                    peak_ref[...] = peak

        @pl.when(pair == 0)
        def _():
            loads[-1].wait()

        pooled = jnp.dot(table_ref[...], counts_ref[pair], preferred_element_type=jnp.float32)
        pooled_ref[2 * pair] = pooled[:, :LANES]
        pooled_ref[2 * pair + 1] = pooled[:, LANES:]
        return carry

    lax.fori_loop(0, len(masks) // 2, count_pair, 0)

    large = jnp.max(peak_ref[...].astype(jnp.float32)) >= EXACT
    flag_ref[0] = large.astype(jnp.int32)

    @pl.when(large)
    def _():
        def redo(index, carry):
            owner = owner_of(index)
            counts = factor_product(
                row_ref[pl.ds(owner, 1), :], sample_ref[pl.ds(owner, 1), :],
                weight_ref[pl.ds(owner, 1), :], count_ref[0, owner], low, span, row_ref.shape[1],
            )
            rest = (counts - counts.astype(jnp.bfloat16).astype(jnp.float32)).astype(jnp.bfloat16)
            for part in range(span):
                spill_ref[part * low : (part + 1) * low, :] = rest[
                    :, part * LANES : (part + 1) * LANES
                ]
            pooled_ref[index] += jnp.dot(
                table_ref[...], spill_ref[...], preferred_element_type=jnp.float32
            )
            copy = pltpu.make_async_copy(spill_ref, low_ref.at[index], sems.at[0])
            copy.start()
            copy.wait()
            return carry

        lax.fori_loop(0, len(masks), redo, 0)


def count_call(masks, send_count, row, sample, weight, table):
    total = len(masks)
    dim_local, row_local = table.shape
    peers, slots = row.shape
    low = math.gcd(row_local, 512)
    span = row_local // low
    hbm = pl.BlockSpec(memory_space=pltpu.HBM)
    vmem = pl.BlockSpec(memory_space=pltpu.VMEM)
    return pl.pallas_call(
        functools.partial(
            count_kernel, masks=masks, low=low, span=span, chunks=-(-slots // CHUNK)
        ),
        in_specs=[hbm] * 5,
        out_specs=[vmem, vmem, hbm, pl.BlockSpec(memory_space=pltpu.SMEM)],
        scratch_shapes=[
            pltpu.SMEM((1, peers), jnp.int32),
            pltpu.VMEM(row.shape, jnp.int32),
            pltpu.VMEM(row.shape, jnp.int32),
            pltpu.VMEM(row.shape, jnp.int32),
            pltpu.VMEM(table.shape, jnp.bfloat16),
            pltpu.VMEM((low, LANES), jnp.bfloat16),
            pltpu.VMEM((row_local, LANES), jnp.bfloat16),
            pltpu.SemaphoreType.DMA((5,)),
        ],
        out_shape=[
            jax.ShapeDtypeStruct((total // 2, row_local, 2 * LANES), jnp.bfloat16),
            jax.ShapeDtypeStruct((total, dim_local, LANES), jnp.float32),
            jax.ShapeDtypeStruct((total, row_local, LANES), jnp.bfloat16),
            jax.ShapeDtypeStruct((1,), jnp.int32),
        ],
        compiler_params=pltpu.CompilerParams(vmem_limit_bytes=VMEM_LIMIT),
        name="counts",
    )(*(pltpu.with_memory_space_constraint(x, pltpu.HBM) for x in (send_count[None], row, sample, weight, table)))


def grad_kernel(*refs, terms, parts, pieces, block, chained, last):
    flag_refs = refs[:parts]
    counts_refs = refs[parts : 2 * parts]
    low_refs = refs[2 * parts : 3 * parts]
    grads = refs[3 * parts : 3 * parts + pieces]
    rest = list(refs[3 * parts + pieces :])
    before_ref = rest.pop(0) if chained else None
    grad_ref = rest.pop(0)
    square_ref = rest.pop(0) if last else None
    spill_ref, sem = rest
    row_local = grad_ref.shape[1]
    lefts = [
        jnp.concatenate([grads[piece][place] for piece, place in term[2:]], axis=1)
        for term in terms
    ]
    for start in range(0, row_local, block):
        rows = slice(start, start + block)
        total = before_ref[:, rows] if chained else None
        for left, (part, pair, *_) in zip(lefts, terms):
            found = lax.dot_general(
                left, counts_refs[part][pair, rows, :], (((1,), (1,)), ((), ())),
                preferred_element_type=jnp.float32,
            )
            total = found if total is None else total + found
        grad_ref[:, rows] = total
        if last:
            square_ref[:, rows] = jnp.sum(total * total, axis=0, keepdims=True)

    for part in range(parts):
        mine = [term for term in terms if term[0] == part]
        if not mine:
            continue

        @pl.when(flag_refs[part][0] > 0)
        def _(part=part, mine=mine):
            for _, pair, *homes in mine:
                for member, (piece, place) in enumerate(homes):
                    copy = pltpu.make_async_copy(low_refs[part].at[2 * pair + member], spill_ref, sem)
                    copy.start()
                    copy.wait()
                    for start in range(0, row_local, block):
                        rows = slice(start, start + block)
                        grad_ref[:, rows] += lax.dot_general(
                            grads[piece][place], spill_ref[rows, :], (((1,), (1,)), ((), ())),
                            preferred_element_type=jnp.float32,
                        )
            if last:
                for start in range(0, row_local, block):
                    rows = slice(start, start + block)
                    final = grad_ref[:, rows]
                    square_ref[:, rows] = jnp.sum(final * final, axis=0, keepdims=True)


def grad_call(terms, flags, counts, lows, grads, before, last):
    parts = len(counts)
    row_local = counts[0].shape[1]
    dim_local = grads[0].shape[1]
    chained = before is not None
    smem = pl.BlockSpec(memory_space=pltpu.SMEM)
    vmem = pl.BlockSpec(memory_space=pltpu.VMEM)
    hbm = pl.BlockSpec(memory_space=pltpu.HBM)
    out = [jax.ShapeDtypeStruct((dim_local, row_local), jnp.float32)]
    if last:
        out.append(jax.ShapeDtypeStruct((1, row_local), jnp.float32))
    return pl.pallas_call(
        functools.partial(
            grad_kernel, terms=terms, parts=parts, pieces=len(grads),
            block=math.gcd(row_local, 512), chained=chained, last=last,
        ),
        in_specs=[smem] * parts + [vmem] * parts + [hbm] * parts + [vmem] * (len(grads) + chained),
        out_specs=[vmem] * len(out),
        out_shape=out,
        scratch_shapes=[pltpu.VMEM((row_local, LANES), jnp.bfloat16), pltpu.SemaphoreType.DMA],
        compiler_params=pltpu.CompilerParams(vmem_limit_bytes=VMEM_LIMIT),
        name="grads",
    )(*flags, *counts, *lows, *grads, *([before] if chained else []))


def flip(value, axis, mask):
    size = lax.axis_size(axis)
    return lax.ppermute(value, axis, [(index, index ^ mask) for index in range(size)])


def plan(peers):
    bits = [1 << place for place in range(peers.bit_length() - 1)]
    gather_bits = bits[-1:] + bits[:-1]
    stages = len(bits)
    blocks = [None] * stages
    phases = [None] * stages
    blocks[-1] = [0]
    for stage in reversed(range(stages)):
        if stage < stages - 1:
            blocks[stage] = phases[stage + 1] + blocks[stage + 1]
        phases[stage] = [bits[stage] ^ mask for mask in blocks[stage]]
    return bits, gather_bits, blocks, phases


def staged(table, grad_pooled, sample, row, weight, send_count):
    bits, gather_bits, blocks, phases = plan(lax.axis_size("rows"))
    stages = len(bits)
    passes = [phases[0], blocks[0]]
    inputs = (send_count, row, sample, weight, table)

    pieces = [grad_pooled[None]]
    homes = {0: (0, 0)}

    def arrived(piece, bit):
        for mask, (index, place) in list(homes.items()):
            base = sum(p.shape[0] for p in pieces[:index]) + place
            homes[mask ^ bit] = (len(pieces), base)
        pieces.append(piece)

    arrived(flip(pieces[0], "rows", gather_bits[0]), gather_bits[0])
    counts0, partial0, low0, flag0 = count_call(passes[0], *inputs)
    partial0, pieces[1] = lax.optimization_barrier((partial0, pieces[1]))
    known = [set(homes)]
    received = [flip(partial0, "rows", bits[0])]
    if stages > 1:
        arrived(flip(jnp.concatenate(pieces), "rows", gather_bits[1]), gather_bits[1])
    known.append(set(homes))
    counts1, partial1, low1, flag1 = count_call(passes[1], *inputs)
    partial1, received[0], pieces[-1] = lax.optimization_barrier(
        (partial1, received[0], pieces[-1])
    )
    total = partial1 + received[0]
    for stage in range(1, stages):
        take = len(phases[stage])
        if stage + 1 < stages:
            arrived(
                flip(jnp.concatenate(pieces), "rows", gather_bits[stage + 1]),
                gather_bits[stage + 1],
            )
        received.append(flip(total[:take], "rows", bits[stage]))
        total = total[take:]
        if stage < stages - 1:
            total = total + received[-1]
        else:
            pooled = total[0] + received[-1][0]

    flags, counts, lows = [flag0, flag1], [counts0, counts1], [low0, low1]
    early, late = [], []
    for part, masks in enumerate(passes):
        for pair in range(len(masks) // 2):
            two = masks[2 * pair : 2 * pair + 2]
            term = (part, pair, homes[two[0]], homes[two[1]])
            (early if set(two) <= known[1] else late).append(term)
    row_grad = None
    if early and late:
        used = 1 + max(home[0] for term in early for home in term[2:])
        (row_grad,) = grad_call(early, flags, counts, lows, pieces[:used], None, False)
    else:
        late = early + late
    row_grad, square = grad_call(late, flags, counts, lows, pieces, row_grad, True)
    return pooled, row_grad, square


def share(square):
    terms = [square]
    mask = lax.axis_size("dims") // 2
    while mask >= 1:
        terms = terms + [flip(term, "dims", mask) for term in terms]
        mask //= 2
    while len(terms) > 1:
        half = len(terms) // 2
        terms = [terms[index] + terms[index + half] for index in range(half)]
    return terms[0]


def update(table, accum, row_grad, square):
    new_accum = accum[None, :] + share(square) / D
    scale = step_size / jnp.sqrt(new_accum)
    new_table = (table.astype(jnp.float32) - row_grad * scale).astype(jnp.bfloat16)
    return new_table, new_accum[0]


def fits(table, grad_pooled, peers):
    return (
        peers & (peers - 1) == 0
        and peers > 2
        and lax.axis_size("dims") & (lax.axis_size("dims") - 1) == 0
        and grad_pooled.shape[2] == LANES
        and peers * table.shape[2] * LANES * 2 <= FAST_BYTES
    )


def shards(table, accum, grad_pooled, sample_slot, row_slot, weight, send_count):
    peers = lax.axis_size("rows")
    if not fits(table, grad_pooled, peers):
        return plain(table, accum, grad_pooled, sample_slot, row_slot, weight, send_count)
    outs = []
    for feature in range(table.shape[0]):
        pooled, row_grad, square = staged(
            table[feature], grad_pooled[feature], sample_slot[feature, 0],
            row_slot[feature, 0], weight[feature, 0], send_count[feature, 0],
        )
        new_table, new_accum = update(table[feature], accum[feature], row_grad, square)
        outs.append((pooled, new_table, new_accum))
    return tuple(jnp.stack(out) for out in zip(*outs))


def plain(table, accum, grad_pooled, sample_slot, row_slot, weight, send_count):
    feat_count, dim_local, row_local = table.shape
    peer_count = lax.axis_size("rows")
    own_samples = grad_pooled.shape[2]
    slot_count = sample_slot.shape[3]
    entry_count = peer_count * slot_count
    block_rows = math.gcd(row_local, 512)
    block_count = row_local // block_rows
    sample_local = sample_slot.reshape(feat_count, peer_count, slot_count)
    row_index = row_slot.reshape(feat_count, peer_count, slot_count)
    flat_rows = row_index.reshape(feat_count, 1, entry_count)
    live_count = send_count.reshape(feat_count, peer_count)
    slot_iota = lax.broadcasted_iota(jnp.int32, (1, 1, slot_count), 2)
    live_mask = slot_iota < live_count[:, :, None]
    weights = jnp.where(live_mask, weight.reshape(feat_count, peer_count, slot_count), 0)
    flat_weights = weights.reshape(feat_count, 1, entry_count).astype(jnp.bfloat16)
    block_iota = lax.broadcasted_iota(jnp.int32, (1, block_rows, 1), 1)

    def lookup_block(carry, block):
        start = block * block_rows
        table_part = lax.dynamic_slice_in_dim(table, start, block_rows, 2)
        selector = (flat_rows == block_iota + start).astype(jnp.bfloat16)
        return (
            carry
            + jnp.einsum("fdr,fre->fde", table_part, selector, preferred_element_type=jnp.float32),
            None,
        )

    looked_up, _ = lax.scan(
        lookup_block,
        jnp.zeros((feat_count, dim_local, entry_count), jnp.float32),
        jnp.arange(block_count, dtype=jnp.int32),
    )
    picked = looked_up.astype(jnp.bfloat16).reshape(feat_count, dim_local, peer_count, slot_count)
    positions = lax.broadcasted_iota(jnp.int32, (1, 1, 1, own_samples), 3)
    onehot = jnp.where(sample_local[..., None] == positions, weights[..., None], 0).astype(
        jnp.bfloat16
    )
    pooled = lax.psum_scatter(
        jnp.einsum("fdnk,fnkj->nfdj", picked, onehot, preferred_element_type=jnp.float32),
        "rows",
        scatter_dimension=0,
        tiled=True,
    ).reshape(feat_count, dim_local, own_samples)
    all_grads = lax.all_gather(grad_pooled, "rows", axis=2, tiled=True)
    all_grads = all_grads.reshape(feat_count, dim_local, peer_count, own_samples)
    selector = (sample_local[..., None] == positions).astype(jnp.bfloat16)
    entry_values = jnp.einsum(
        "fdnj,fnkj->fdnk", all_grads, selector, preferred_element_type=jnp.float32
    ).astype(jnp.bfloat16)
    entry_flat = entry_values.reshape(feat_count, dim_local, entry_count)

    def gradient_block(block):
        start = block * block_rows
        weighted = jnp.where(flat_rows == block_iota + start, flat_weights, 0)
        return jnp.einsum("fde,fre->fdr", entry_flat, weighted, preferred_element_type=jnp.float32)

    grad_blocks = lax.map(gradient_block, jnp.arange(block_count, dtype=jnp.int32))
    row_grad = jnp.moveaxis(grad_blocks, 0, 2).reshape(feat_count, dim_local, row_local)
    squares = jnp.sum(row_grad * row_grad, axis=1)
    norm_total = lax.psum(squares, "dims")
    new_accum = accum + norm_total / D
    new_table = (
        table.astype(jnp.float32) - step_size * row_grad / jnp.sqrt(new_accum)[:, None, :]
    ).astype(jnp.bfloat16)
    return (pooled, new_table, new_accum)


def solution(mesh):
    return jax.shard_map(
        shards,
        mesh=mesh,
        in_specs=(
            P(None, "dims", "rows"),
            P(None, "rows"),
            P(None, "dims", "rows"),
            P(None, "rows", None, None),
            P(None, "rows", None, None),
            P(None, "rows", None, None),
            P(None, "rows", None),
        ),
        out_specs=(P(None, "dims", "rows"), P(None, "dims", "rows"), P(None, "rows")),
        check_vma=False,
    )
```

```python
import functools
import math

import jax
import jax.numpy as jnp
from jax import lax
from jax.experimental import pallas as pl
from jax.experimental.pallas import tpu as pltpu
from jax.sharding import PartitionSpec as P


D = 256


step_size = 0.3


LANES = 128
CHUNK = 256
NARROW = jnp.float8_e4m3fn
EXACT = 256.0
FAST_BYTES = 24 << 20
VMEM_LIMIT = 16 << 20


def factor_product(row, sample, weight, count, low, span, depth):
    row = row[:, :depth]
    slot = lax.broadcasted_iota(jnp.int32, row.shape, 1)
    live = jnp.where(slot < count, weight[:, :depth], 0).astype(jnp.bfloat16)
    left_key = (row % low).astype(jnp.int16)
    right_key = ((row // low) * LANES + sample[:, :depth]).astype(jnp.int16)
    left_iota = lax.broadcasted_iota(jnp.int16, (low, depth), 0)
    right_iota = lax.broadcasted_iota(jnp.int16, (span * LANES, depth), 0)
    zero = jnp.bfloat16(0)
    left = jnp.where(left_iota == left_key, live, zero).astype(NARROW)
    right = jnp.where(right_iota == right_key, jnp.bfloat16(1), zero).astype(NARROW)
    return lax.dot_general(
        left, right, (((1,), (1,)), ((), ())), preferred_element_type=jnp.float32
    )


def count_kernel(*refs, first, masks, low, span, chunks):
    sources = refs[:5]
    extra = 6 if first else 0
    if first:
        grad_hbm = refs[5]
        refs = refs[6:]
    else:
        refs = refs[5:]
    counts_ref, pooled_ref, low_ref, peak_ref = refs[:4]
    held = refs[4 : 4 + extra]
    count_ref, most_ref, spill_ref, sems = refs[4 + extra :]
    loads = []
    if first:
        loads = [
            pltpu.make_async_copy(source, target, sems.at[index])
            for index, (source, target) in enumerate(zip((*sources, grad_hbm), held))
        ]
        for load in loads:
            load.start()
        _, row_ref, sample_ref, weight_ref, table_ref = held[:5]
        scalars = pltpu.make_async_copy(sources[0], count_ref, sems.at[6])
    else:
        _, row_ref, sample_ref, weight_ref, table_ref = sources
        scalars = pltpu.make_async_copy(sources[0], count_ref, sems.at[6])
    scalars.start()
    me = lax.axis_index("rows")
    most_ref[...] = jnp.zeros_like(most_ref)
    for load in loads[:4]:
        load.wait()
    scalars.wait()

    def owner_of(index):
        owner = me ^ masks[0]
        for place, mask in enumerate(masks[1:], 1):
            owner = jnp.where(index == place, me ^ mask, owner)
        return owner

    def count_pair(pair, carry):
        for member in range(2):
            owner = owner_of(2 * pair + member)
            count = count_ref[0, owner]
            row = row_ref[pl.ds(owner, 1), :]
            sample = sample_ref[pl.ds(owner, 1), :]
            weight = weight_ref[pl.ds(owner, 1), :]
            needed = jnp.maximum((count + CHUNK - 1) // CHUNK, 1)
            for chunk in range(1, chunks + 1):

                @pl.when(needed == chunk)
                def _(chunk=chunk):
                    depth = min(chunk * CHUNK, row.shape[1])
                    counts = factor_product(row, sample, weight, count, low, span, depth)
                    counts = counts.astype(jnp.bfloat16)
                    peak = most_ref[...]
                    for part in range(span):
                        piece = counts[:, part * LANES : (part + 1) * LANES]
                        counts_ref[
                            pair, part * low : (part + 1) * low,
                            member * LANES : (member + 1) * LANES,
                        ] = piece
                        peak = jnp.maximum(peak, piece)
                    most_ref[...] = peak

        if first:

            @pl.when(pair == 0)
            def _():
                for load in loads[4:]:
                    load.wait()

        pooled = jnp.dot(table_ref[...], counts_ref[pair], preferred_element_type=jnp.float32)
        pooled_ref[2 * pair] = pooled[:, :LANES]
        pooled_ref[2 * pair + 1] = pooled[:, LANES:]
        return carry

    lax.fori_loop(0, len(masks) // 2, count_pair, 0)

    most = most_ref[0:16, :]
    for start in range(16, low, 16):
        most = jnp.maximum(most, most_ref[start : start + 16, :])
    peak_ref[...] = most.astype(jnp.float32)

    @pl.when(jnp.max(peak_ref[...]) >= EXACT)
    def _():
        def redo(index, carry):
            owner = owner_of(index)
            counts = factor_product(
                row_ref[pl.ds(owner, 1), :], sample_ref[pl.ds(owner, 1), :],
                weight_ref[pl.ds(owner, 1), :], count_ref[0, owner], low, span, row_ref.shape[1],
            )
            rest = (counts - counts.astype(jnp.bfloat16).astype(jnp.float32)).astype(jnp.bfloat16)
            for part in range(span):
                spill_ref[part * low : (part + 1) * low, :] = rest[
                    :, part * LANES : (part + 1) * LANES
                ]
            pooled_ref[index] += jnp.dot(
                table_ref[...], spill_ref[...], preferred_element_type=jnp.float32
            )
            copy = pltpu.make_async_copy(spill_ref, low_ref.at[index], sems.at[0])
            copy.start()
            copy.wait()
            return carry

        lax.fori_loop(0, len(masks), redo, 0)


def count_call(masks, operands, grad, peers):
    first = grad is not None
    _, row, _, _, table = operands
    total = len(masks)
    dim_local, row_local = table.shape
    slots = row.shape[1]
    low = math.gcd(row_local, 512)
    span = row_local // low
    hbm = pl.BlockSpec(memory_space=pltpu.HBM)
    vmem = pl.BlockSpec(memory_space=pltpu.VMEM)
    if first:
        arguments = [
            pltpu.with_memory_space_constraint(value, pltpu.HBM) for value in (*operands, grad)
        ]
    else:
        arguments = list(operands)
    held = [jax.ShapeDtypeStruct(value.shape, value.dtype) for value in arguments] if first else []
    return pl.pallas_call(
        functools.partial(
            count_kernel, first=first, masks=masks, low=low, span=span, chunks=-(-slots // CHUNK)
        ),
        in_specs=[hbm if first else vmem] * len(arguments),
        out_specs=[vmem, vmem, hbm, vmem] + [vmem] * len(held),
        scratch_shapes=[
            pltpu.SMEM((1, peers), jnp.int32),
            pltpu.VMEM((low, LANES), jnp.bfloat16),
            pltpu.VMEM((row_local, LANES), jnp.bfloat16),
            pltpu.SemaphoreType.DMA((7,)),
        ],
        out_shape=[
            jax.ShapeDtypeStruct((total // 2, row_local, 2 * LANES), jnp.bfloat16),
            jax.ShapeDtypeStruct((total, dim_local, LANES), jnp.float32),
            jax.ShapeDtypeStruct((total, row_local, LANES), jnp.bfloat16),
            jax.ShapeDtypeStruct((16, LANES), jnp.float32),
        ]
        + held,
        compiler_params=pltpu.CompilerParams(vmem_limit_bytes=VMEM_LIMIT),
        name="counts",
    )(*arguments)


def grad_kernel(*refs, terms, parts, pieces, block, chained, last):
    flag_refs = refs[:parts]
    counts_refs = refs[parts : 2 * parts]
    low_refs = refs[2 * parts : 3 * parts]
    grads = refs[3 * parts : 3 * parts + pieces]
    rest = list(refs[3 * parts + pieces :])
    before_ref = rest.pop(0) if chained else None
    grad_ref = rest.pop(0)
    square_ref = rest.pop(0) if last else None
    spill_ref, sem = rest
    row_local = grad_ref.shape[1]
    lefts = [
        jnp.concatenate([grads[piece][place] for piece, place in term[2:]], axis=1)
        for term in terms
    ]
    for start in range(0, row_local, block):
        rows = slice(start, start + block)
        total = before_ref[:, rows] if chained else None
        for left, (part, pair, *_) in zip(lefts, terms):
            found = lax.dot_general(
                left, counts_refs[part][pair, rows, :], (((1,), (1,)), ((), ())),
                preferred_element_type=jnp.float32,
            )
            total = found if total is None else total + found
        grad_ref[:, rows] = total
        if last:
            square_ref[:, rows] = jnp.sum(total * total, axis=0, keepdims=True)

    for part in range(parts):
        mine = [term for term in terms if term[0] == part]
        if not mine:
            continue

        @pl.when(jnp.max(flag_refs[part][...]) >= EXACT)
        def _(part=part, mine=mine):
            for _, pair, *homes in mine:
                for member, (piece, place) in enumerate(homes):
                    copy = pltpu.make_async_copy(low_refs[part].at[2 * pair + member], spill_ref, sem)
                    copy.start()
                    copy.wait()
                    for start in range(0, row_local, block):
                        rows = slice(start, start + block)
                        grad_ref[:, rows] += lax.dot_general(
                            grads[piece][place], spill_ref[rows, :], (((1,), (1,)), ((), ())),
                            preferred_element_type=jnp.float32,
                        )
            if last:
                for start in range(0, row_local, block):
                    rows = slice(start, start + block)
                    final = grad_ref[:, rows]
                    square_ref[:, rows] = jnp.sum(final * final, axis=0, keepdims=True)


def grad_call(terms, flags, counts, lows, grads, before, last):
    parts = len(counts)
    row_local = counts[0].shape[1]
    dim_local = grads[0].shape[1]
    chained = before is not None
    vmem = pl.BlockSpec(memory_space=pltpu.VMEM)
    hbm = pl.BlockSpec(memory_space=pltpu.HBM)
    out = [jax.ShapeDtypeStruct((dim_local, row_local), jnp.float32)]
    if last:
        out.append(jax.ShapeDtypeStruct((1, row_local), jnp.float32))
    return pl.pallas_call(
        functools.partial(
            grad_kernel, terms=terms, parts=parts, pieces=len(grads),
            block=math.gcd(row_local, 512), chained=chained, last=last,
        ),
        in_specs=[vmem] * parts + [vmem] * parts + [hbm] * parts + [vmem] * (len(grads) + chained),
        out_specs=[vmem] * len(out),
        out_shape=out,
        scratch_shapes=[pltpu.VMEM((row_local, LANES), jnp.bfloat16), pltpu.SemaphoreType.DMA],
        compiler_params=pltpu.CompilerParams(vmem_limit_bytes=VMEM_LIMIT),
        name="grads",
    )(*flags, *counts, *lows, *grads, *([before] if chained else []))


def flip(value, axis, mask):
    size = lax.axis_size(axis)
    return lax.ppermute(value, axis, [(index, index ^ mask) for index in range(size)])


def plan(peers):
    bits = [1 << place for place in range(peers.bit_length() - 1)]
    gather_bits = bits[-1:] + bits[:-1]
    stages = len(bits)
    blocks = [None] * stages
    phases = [None] * stages
    blocks[-1] = [0]
    for stage in reversed(range(stages)):
        if stage < stages - 1:
            blocks[stage] = phases[stage + 1] + blocks[stage + 1]
        phases[stage] = [bits[stage] ^ mask for mask in blocks[stage]]
    return bits, gather_bits, blocks, phases


def staged(table, grad_pooled, sample, row, weight, send_count):
    bits, gather_bits, blocks, phases = plan(lax.axis_size("rows"))
    stages = len(bits)
    passes = [phases[0], blocks[0]]
    peers = lax.axis_size("rows")

    pieces = [grad_pooled[None]]
    homes = {0: (0, 0)}

    def arrived(piece, bit):
        for mask, (index, place) in list(homes.items()):
            base = sum(p.shape[0] for p in pieces[:index]) + place
            homes[mask ^ bit] = (len(pieces), base)
        pieces.append(piece)

    arrived(flip(pieces[0], "rows", gather_bits[0]), gather_bits[0])
    counts0, partial0, low0, flag0, *held = count_call(
        passes[0], (send_count[None], row, sample, weight, table), pieces[0], peers
    )
    pieces[0] = held.pop()
    partial0, pieces[1] = lax.optimization_barrier((partial0, pieces[1]))
    known = [set(homes)]
    received = [flip(partial0, "rows", bits[0])]
    if stages > 1:
        arrived(flip(jnp.concatenate(pieces), "rows", gather_bits[1]), gather_bits[1])
    known.append(set(homes))
    counts1, partial1, low1, flag1 = count_call(passes[1], tuple(held), None, peers)
    partial1, received[0], pieces[-1] = lax.optimization_barrier(
        (partial1, received[0], pieces[-1])
    )
    total = partial1 + received[0]
    for stage in range(1, stages):
        take = len(phases[stage])
        if stage + 1 < stages:
            arrived(
                flip(jnp.concatenate(pieces), "rows", gather_bits[stage + 1]),
                gather_bits[stage + 1],
            )
        received.append(flip(total[:take], "rows", bits[stage]))
        total = total[take:]
        if stage < stages - 1:
            total = total + received[-1]

    flags, counts, lows = [flag0, flag1], [counts0, counts1], [low0, low1]
    early, late = [], []
    for part, masks in enumerate(passes):
        for pair in range(len(masks) // 2):
            two = masks[2 * pair : 2 * pair + 2]
            term = (part, pair, homes[two[0]], homes[two[1]])
            (early if set(two) <= known[1] else late).append(term)
    row_grad = None
    if early and late:
        used = 1 + max(home[0] for term in early for home in term[2:])
        (row_grad,) = grad_call(early, flags, counts, lows, pieces[:used], None, False)
    else:
        late = early + late
    row_grad, square = grad_call(late, flags, counts, lows, pieces, row_grad, True)
    return (total, received[-1]), row_grad, square


def share(square):
    terms = [square]
    mask = lax.axis_size("dims") // 2
    while mask >= 1:
        terms = terms + [flip(term, "dims", mask) for term in terms]
        mask //= 2
    return terms


def update_kernel(*refs, count, block):
    terms = refs[:count]
    accum_ref, table_ref, grad_ref, own_ref, other_ref = refs[count : count + 5]
    pooled_hbm, table_hbm, accum_hbm, pooled_ref, new_ref, total_ref, sems = refs[count + 5 :]
    copies = [pltpu.make_async_copy(pooled_ref, pooled_hbm, sems.at[0])]
    pooled_ref[...] = own_ref[...] + other_ref[...]
    copies[0].start()
    row_local = grad_ref.shape[1]
    for index, start in enumerate(range(0, row_local, block)):
        rows = slice(start, start + block)
        sums = [term[:, rows] for term in terms]
        while len(sums) > 1:
            half = len(sums) // 2
            sums = [sums[place] + sums[place + half] for place in range(half)]
        total = accum_ref[:, rows] + sums[0] / D
        total_ref[:, rows] = total
        scale = step_size / jnp.sqrt(total)
        new_ref[:, rows] = (
            table_ref[:, rows].astype(jnp.float32) - grad_ref[:, rows] * scale
        ).astype(jnp.bfloat16)
        copies.append(
            pltpu.make_async_copy(
                new_ref.at[:, pl.ds(start, block)], table_hbm.at[:, pl.ds(start, block)],
                sems.at[1 + index],
            )
        )
        copies[-1].start()
    copies.append(pltpu.make_async_copy(total_ref, accum_hbm, sems.at[len(copies)]))
    copies[-1].start()
    for copy in copies:
        copy.wait()


def update(table, accum, row_grad, square, sums):
    terms = share(square)
    row_local = table.shape[1]
    block = math.gcd(row_local, 1024)
    hbm = pl.BlockSpec(memory_space=pltpu.HBM)
    vmem = pl.BlockSpec(memory_space=pltpu.VMEM)
    pooled, new_table, new_accum = pl.pallas_call(
        functools.partial(update_kernel, count=len(terms), block=block),
        in_specs=[vmem] * (len(terms) + 5),
        out_specs=[hbm] * 3,
        out_shape=[
            jax.ShapeDtypeStruct(sums[0].shape, jnp.float32),
            jax.ShapeDtypeStruct(table.shape, table.dtype),
            jax.ShapeDtypeStruct((1, row_local), jnp.float32),
        ],
        scratch_shapes=[
            pltpu.VMEM(sums[0].shape, jnp.float32),
            pltpu.VMEM(table.shape, table.dtype),
            pltpu.VMEM((1, row_local), jnp.float32),
            pltpu.SemaphoreType.DMA((row_local // block + 2,)),
        ],
        compiler_params=pltpu.CompilerParams(vmem_limit_bytes=VMEM_LIMIT),
        name="update",
    )(*terms, accum[None], table, row_grad, *sums)
    return pooled[0], new_table, new_accum[0]


def fits(table, grad_pooled, peers):
    return (
        peers & (peers - 1) == 0
        and peers > 2
        and lax.axis_size("dims") & (lax.axis_size("dims") - 1) == 0
        and grad_pooled.shape[2] == LANES
        and peers * table.shape[2] * LANES * 2 <= FAST_BYTES
    )


def shards(table, accum, grad_pooled, sample_slot, row_slot, weight, send_count):
    peers = lax.axis_size("rows")
    if not fits(table, grad_pooled, peers):
        return plain(table, accum, grad_pooled, sample_slot, row_slot, weight, send_count)
    outs = []
    for feature in range(table.shape[0]):
        sums, row_grad, square = staged(
            table[feature], grad_pooled[feature], sample_slot[feature, 0],
            row_slot[feature, 0], weight[feature, 0], send_count[feature, 0],
        )
        outs.append(update(table[feature], accum[feature], row_grad, square, sums))
    return tuple(jnp.stack(out) for out in zip(*outs))


def plain(table, accum, grad_pooled, sample_slot, row_slot, weight, send_count):
    feat_count, dim_local, row_local = table.shape
    peer_count = lax.axis_size("rows")
    own_samples = grad_pooled.shape[2]
    slot_count = sample_slot.shape[3]
    entry_count = peer_count * slot_count
    block_rows = math.gcd(row_local, 512)
    block_count = row_local // block_rows
    sample_local = sample_slot.reshape(feat_count, peer_count, slot_count)
    row_index = row_slot.reshape(feat_count, peer_count, slot_count)
    flat_rows = row_index.reshape(feat_count, 1, entry_count)
    live_count = send_count.reshape(feat_count, peer_count)
    slot_iota = lax.broadcasted_iota(jnp.int32, (1, 1, slot_count), 2)
    live_mask = slot_iota < live_count[:, :, None]
    weights = jnp.where(live_mask, weight.reshape(feat_count, peer_count, slot_count), 0)
    flat_weights = weights.reshape(feat_count, 1, entry_count).astype(jnp.bfloat16)
    block_iota = lax.broadcasted_iota(jnp.int32, (1, block_rows, 1), 1)

    def lookup_block(carry, block):
        start = block * block_rows
        table_part = lax.dynamic_slice_in_dim(table, start, block_rows, 2)
        selector = (flat_rows == block_iota + start).astype(jnp.bfloat16)
        return (
            carry
            + jnp.einsum("fdr,fre->fde", table_part, selector, preferred_element_type=jnp.float32),
            None,
        )

    looked_up, _ = lax.scan(
        lookup_block,
        jnp.zeros((feat_count, dim_local, entry_count), jnp.float32),
        jnp.arange(block_count, dtype=jnp.int32),
    )
    picked = looked_up.astype(jnp.bfloat16).reshape(feat_count, dim_local, peer_count, slot_count)
    positions = lax.broadcasted_iota(jnp.int32, (1, 1, 1, own_samples), 3)
    onehot = jnp.where(sample_local[..., None] == positions, weights[..., None], 0).astype(
        jnp.bfloat16
    )
    pooled = lax.psum_scatter(
        jnp.einsum("fdnk,fnkj->nfdj", picked, onehot, preferred_element_type=jnp.float32),
        "rows",
        scatter_dimension=0,
        tiled=True,
    ).reshape(feat_count, dim_local, own_samples)
    all_grads = lax.all_gather(grad_pooled, "rows", axis=2, tiled=True)
    all_grads = all_grads.reshape(feat_count, dim_local, peer_count, own_samples)
    selector = (sample_local[..., None] == positions).astype(jnp.bfloat16)
    entry_values = jnp.einsum(
        "fdnj,fnkj->fdnk", all_grads, selector, preferred_element_type=jnp.float32
    ).astype(jnp.bfloat16)
    entry_flat = entry_values.reshape(feat_count, dim_local, entry_count)

    def gradient_block(block):
        start = block * block_rows
        weighted = jnp.where(flat_rows == block_iota + start, flat_weights, 0)
        return jnp.einsum("fde,fre->fdr", entry_flat, weighted, preferred_element_type=jnp.float32)

    grad_blocks = lax.map(gradient_block, jnp.arange(block_count, dtype=jnp.int32))
    row_grad = jnp.moveaxis(grad_blocks, 0, 2).reshape(feat_count, dim_local, row_local)
    squares = jnp.sum(row_grad * row_grad, axis=1)
    norm_total = lax.psum(squares, "dims")
    new_accum = accum + norm_total / D
    new_table = (
        table.astype(jnp.float32) - step_size * row_grad / jnp.sqrt(new_accum)[:, None, :]
    ).astype(jnp.bfloat16)
    return (pooled, new_table, new_accum)


def solution(mesh):
    return jax.shard_map(
        shards,
        mesh=mesh,
        in_specs=(
            P(None, "dims", "rows"),
            P(None, "rows"),
            P(None, "dims", "rows"),
            P(None, "rows", None, None),
            P(None, "rows", None, None),
            P(None, "rows", None, None),
            P(None, "rows", None),
        ),
        out_specs=(P(None, "dims", "rows"), P(None, "dims", "rows"), P(None, "rows")),
        check_vma=False,
    )
```

```python
import functools
import math

import jax
import jax.numpy as jnp
from jax import lax
from jax.experimental import pallas as pl
from jax.experimental.pallas import tpu as pltpu
from jax.sharding import PartitionSpec as P


D = 256


step_size = 0.3


LANES = 128
CHUNK = 256
NARROW = jnp.float8_e4m3fn
EXACT = 256.0
FAST_BYTES = 24 << 20
VMEM_LIMIT = 16 << 20


def factor_product(row, sample, weight, count, low, span, depth):
    row = row[:, :depth]
    slot = lax.broadcasted_iota(jnp.int32, row.shape, 1)
    live = jnp.where(slot < count, weight[:, :depth], 0).astype(jnp.bfloat16)
    left_key = (row % low).astype(jnp.int16)
    right_key = ((row // low) * LANES + sample[:, :depth]).astype(jnp.int16)
    left_iota = lax.broadcasted_iota(jnp.int16, (low, depth), 0)
    right_iota = lax.broadcasted_iota(jnp.int16, (span * LANES, depth), 0)
    zero = jnp.bfloat16(0)
    left = jnp.where(left_iota == left_key, live, zero).astype(NARROW)
    right = jnp.where(right_iota == right_key, jnp.bfloat16(1), zero).astype(NARROW)
    return lax.dot_general(
        left, right, (((1,), (1,)), ((), ())), preferred_element_type=jnp.float32
    )


def count_kernel(*refs, first, masks, low, span, chunks):
    sources = refs[:5]
    extra = 6 if first else 0
    if first:
        grad_hbm = refs[5]
        refs = refs[6:]
    else:
        refs = refs[5:]
    counts_ref, out_ref, low_ref, peak_ref = refs[:4]
    held = refs[4 : 4 + extra]
    count_ref, most_ref, spill_ref, sum_ref, sems = refs[4 + extra :]
    pooled_ref = sum_ref if first else out_ref
    loads = []
    if first:
        loads = [
            pltpu.make_async_copy(source, target, sems.at[index])
            for index, (source, target) in enumerate(zip((*sources, grad_hbm), held))
        ]
        for load in loads:
            load.start()
        _, row_ref, sample_ref, weight_ref, table_ref = held[:5]
        scalars = pltpu.make_async_copy(sources[0], count_ref, sems.at[6])
    else:
        _, row_ref, sample_ref, weight_ref, table_ref = sources
        scalars = pltpu.make_async_copy(sources[0], count_ref, sems.at[6])
    scalars.start()
    me = lax.axis_index("rows")
    most_ref[...] = jnp.zeros_like(most_ref)
    for load in loads[:4]:
        load.wait()
    scalars.wait()

    def owner_of(index):
        owner = me ^ masks[0]
        for place, mask in enumerate(masks[1:], 1):
            owner = jnp.where(index == place, me ^ mask, owner)
        return owner

    def count_pair(pair, carry):
        for member in range(2):
            owner = owner_of(2 * pair + member)
            count = count_ref[0, owner]
            row = row_ref[pl.ds(owner, 1), :]
            sample = sample_ref[pl.ds(owner, 1), :]
            weight = weight_ref[pl.ds(owner, 1), :]
            needed = jnp.maximum((count + CHUNK - 1) // CHUNK, 1)
            for chunk in range(1, chunks + 1):

                @pl.when(needed == chunk)
                def _(chunk=chunk):
                    depth = min(chunk * CHUNK, row.shape[1])
                    counts = factor_product(row, sample, weight, count, low, span, depth)
                    counts = counts.astype(jnp.bfloat16)
                    peak = most_ref[...]
                    for part in range(span):
                        piece = counts[:, part * LANES : (part + 1) * LANES]
                        counts_ref[
                            pair, part * low : (part + 1) * low,
                            member * LANES : (member + 1) * LANES,
                        ] = piece
                        peak = jnp.maximum(peak, piece)
                    most_ref[...] = peak

        if first:

            @pl.when(pair == 0)
            def _():
                for load in loads[4:]:
                    load.wait()

        pooled = jnp.dot(table_ref[...], counts_ref[pair], preferred_element_type=jnp.float32)
        pooled_ref[2 * pair] = pooled[:, :LANES]
        pooled_ref[2 * pair + 1] = pooled[:, LANES:]
        return carry

    lax.fori_loop(0, len(masks) // 2, count_pair, 0)

    most = most_ref[0:16, :]
    for start in range(16, low, 16):
        most = jnp.maximum(most, most_ref[start : start + 16, :])
    peak_ref[...] = most.astype(jnp.float32)

    @pl.when(jnp.max(peak_ref[...]) >= EXACT)
    def _():
        def redo(index, carry):
            owner = owner_of(index)
            counts = factor_product(
                row_ref[pl.ds(owner, 1), :], sample_ref[pl.ds(owner, 1), :],
                weight_ref[pl.ds(owner, 1), :], count_ref[0, owner], low, span, row_ref.shape[1],
            )
            rest = (counts - counts.astype(jnp.bfloat16).astype(jnp.float32)).astype(jnp.bfloat16)
            for part in range(span):
                spill_ref[part * low : (part + 1) * low, :] = rest[
                    :, part * LANES : (part + 1) * LANES
                ]
            pooled_ref[index] += jnp.dot(
                table_ref[...], spill_ref[...], preferred_element_type=jnp.float32
            )
            copy = pltpu.make_async_copy(spill_ref, low_ref.at[index], sems.at[0])
            copy.start()
            copy.wait()
            return carry

        lax.fori_loop(0, len(masks), redo, 0)

    if first:
        sums = sum_ref[...]
        head = sums.astype(jnp.bfloat16)
        out_ref[: len(masks)] = head
        out_ref[len(masks) :] = (sums - head.astype(jnp.float32)).astype(jnp.bfloat16)


def count_call(masks, operands, grad, peers):
    first = grad is not None
    _, row, _, _, table = operands
    total = len(masks)
    dim_local, row_local = table.shape
    slots = row.shape[1]
    low = math.gcd(row_local, 512)
    span = row_local // low
    hbm = pl.BlockSpec(memory_space=pltpu.HBM)
    vmem = pl.BlockSpec(memory_space=pltpu.VMEM)
    if first:
        arguments = [
            pltpu.with_memory_space_constraint(value, pltpu.HBM) for value in (*operands, grad)
        ]
    else:
        arguments = list(operands)
    held = [jax.ShapeDtypeStruct(value.shape, value.dtype) for value in arguments] if first else []
    return pl.pallas_call(
        functools.partial(
            count_kernel, first=first, masks=masks, low=low, span=span, chunks=-(-slots // CHUNK)
        ),
        in_specs=[hbm if first else vmem] * len(arguments),
        out_specs=[vmem, vmem, hbm, vmem] + [vmem] * len(held),
        scratch_shapes=[
            pltpu.SMEM((1, peers), jnp.int32),
            pltpu.VMEM((low, LANES), jnp.bfloat16),
            pltpu.VMEM((row_local, LANES), jnp.bfloat16),
            pltpu.VMEM((total, dim_local, LANES), jnp.float32),
            pltpu.SemaphoreType.DMA((7,)),
        ],
        out_shape=[
            jax.ShapeDtypeStruct((total // 2, row_local, 2 * LANES), jnp.bfloat16),
            jax.ShapeDtypeStruct((2 * total, dim_local, LANES), jnp.bfloat16)
            if first
            else jax.ShapeDtypeStruct((total, dim_local, LANES), jnp.float32),
            jax.ShapeDtypeStruct((total, row_local, LANES), jnp.bfloat16),
            jax.ShapeDtypeStruct((16, LANES), jnp.float32),
        ]
        + held,
        compiler_params=pltpu.CompilerParams(vmem_limit_bytes=VMEM_LIMIT),
        name="counts",
    )(*arguments)


def grad_kernel(*refs, terms, parts, pieces, block, chained, last):
    flag_refs = refs[:parts]
    counts_refs = refs[parts : 2 * parts]
    low_refs = refs[2 * parts : 3 * parts]
    grads = refs[3 * parts : 3 * parts + pieces]
    rest = list(refs[3 * parts + pieces :])
    before_ref = rest.pop(0) if chained else None
    grad_ref = rest.pop(0)
    square_ref = rest.pop(0) if last else None
    spill_ref, sem = rest
    row_local = grad_ref.shape[1]
    lefts = [
        jnp.concatenate([grads[piece][place] for piece, place in term[2:]], axis=1)
        for term in terms
    ]
    for start in range(0, row_local, block):
        rows = slice(start, start + block)
        total = before_ref[:, rows] if chained else None
        for left, (part, pair, *_) in zip(lefts, terms):
            found = lax.dot_general(
                left, counts_refs[part][pair, rows, :], (((1,), (1,)), ((), ())),
                preferred_element_type=jnp.float32,
            )
            total = found if total is None else total + found
        grad_ref[:, rows] = total
        if last:
            square_ref[:, rows] = jnp.sum(total * total, axis=0, keepdims=True)

    for part in range(parts):
        mine = [term for term in terms if term[0] == part]
        if not mine:
            continue

        @pl.when(jnp.max(flag_refs[part][...]) >= EXACT)
        def _(part=part, mine=mine):
            for _, pair, *homes in mine:
                for member, (piece, place) in enumerate(homes):
                    copy = pltpu.make_async_copy(low_refs[part].at[2 * pair + member], spill_ref, sem)
                    copy.start()
                    copy.wait()
                    for start in range(0, row_local, block):
                        rows = slice(start, start + block)
                        grad_ref[:, rows] += lax.dot_general(
                            grads[piece][place], spill_ref[rows, :], (((1,), (1,)), ((), ())),
                            preferred_element_type=jnp.float32,
                        )
            if last:
                for start in range(0, row_local, block):
                    rows = slice(start, start + block)
                    final = grad_ref[:, rows]
                    square_ref[:, rows] = jnp.sum(final * final, axis=0, keepdims=True)


def grad_call(terms, flags, counts, lows, grads, before, last):
    parts = len(counts)
    row_local = counts[0].shape[1]
    dim_local = grads[0].shape[1]
    chained = before is not None
    vmem = pl.BlockSpec(memory_space=pltpu.VMEM)
    hbm = pl.BlockSpec(memory_space=pltpu.HBM)
    out = [jax.ShapeDtypeStruct((dim_local, row_local), jnp.float32)]
    if last:
        out.append(jax.ShapeDtypeStruct((1, row_local), jnp.float32))
    return pl.pallas_call(
        functools.partial(
            grad_kernel, terms=terms, parts=parts, pieces=len(grads),
            block=math.gcd(row_local, 512), chained=chained, last=last,
        ),
        in_specs=[vmem] * parts + [vmem] * parts + [hbm] * parts + [vmem] * (len(grads) + chained),
        out_specs=[vmem] * len(out),
        out_shape=out,
        scratch_shapes=[pltpu.VMEM((row_local, LANES), jnp.bfloat16), pltpu.SemaphoreType.DMA],
        compiler_params=pltpu.CompilerParams(vmem_limit_bytes=VMEM_LIMIT),
        name="grads",
    )(*flags, *counts, *lows, *grads, *([before] if chained else []))


def flip(value, axis, mask):
    size = lax.axis_size(axis)
    return lax.ppermute(value, axis, [(index, index ^ mask) for index in range(size)])


def plan(peers):
    bits = [1 << place for place in range(peers.bit_length() - 1)]
    gather_bits = bits[-1:] + bits[:-1]
    stages = len(bits)
    blocks = [None] * stages
    phases = [None] * stages
    blocks[-1] = [0]
    for stage in reversed(range(stages)):
        if stage < stages - 1:
            blocks[stage] = phases[stage + 1] + blocks[stage + 1]
        phases[stage] = [bits[stage] ^ mask for mask in blocks[stage]]
    return bits, gather_bits, blocks, phases


def staged(table, grad_pooled, sample, row, weight, send_count):
    bits, gather_bits, blocks, phases = plan(lax.axis_size("rows"))
    stages = len(bits)
    passes = [phases[0], blocks[0]]
    peers = lax.axis_size("rows")

    pieces = [grad_pooled[None]]
    homes = [(0, (0, 0))]

    def gathered():
        sizes = [sum(home[0] == index for _, home in homes) for index in range(len(pieces))]
        return [piece[:size] for piece, size in zip(pieces, sizes)]

    def arrived(piece, bit):
        homes.extend(
            [(mask ^ bit, (len(pieces), place)) for place, (mask, _) in enumerate(homes)]
        )
        pieces.append(piece)

    arrived(flip(pieces[0], "rows", gather_bits[0]), gather_bits[0])
    counts0, halves, low0, flag0, *held = count_call(
        passes[0], (send_count[None], row, sample, weight, table), pieces[0], peers
    )
    pieces[0] = held.pop()
    halves, pieces[1] = lax.optimization_barrier((halves, pieces[1]))
    sent = len(homes)
    message = flip(jnp.concatenate(gathered() + [halves]), "rows", bits[0])
    arrived(message, gather_bits[1])
    known = {mask for mask, _ in homes}
    counts1, partial1, low1, flag1 = count_call(passes[1], tuple(held), None, peers)
    partial1, message = lax.optimization_barrier((partial1, message))
    pieces[-1] = message
    half = len(passes[0])
    total = partial1 + (
        message[sent : sent + half].astype(jnp.float32)
        + message[sent + half :].astype(jnp.float32)
    )
    for stage in range(1, stages):
        take = len(phases[stage])
        if stage + 1 < stages:
            arrived(
                flip(jnp.concatenate(gathered()), "rows", gather_bits[stage + 1]),
                gather_bits[stage + 1],
            )
        incoming = flip(total[:take], "rows", bits[stage])
        total = total[take:]
        if stage < stages - 1:
            total = total + incoming

    flags, counts, lows = [flag0, flag1], [counts0, counts1], [low0, low1]
    spots = dict(homes)
    early, late = [], []
    for part, masks in enumerate(passes):
        for pair in range(len(masks) // 2):
            two = masks[2 * pair : 2 * pair + 2]
            term = (part, pair, spots[two[0]], spots[two[1]])
            (early if set(two) <= known else late).append(term)
    row_grad = None
    if early and late:
        used = 1 + max(home[0] for term in early for home in term[2:])
        (row_grad,) = grad_call(early, flags, counts, lows, pieces[:used], None, False)
    else:
        late = early + late
    row_grad, square = grad_call(late, flags, counts, lows, pieces, row_grad, True)
    return (total, incoming), row_grad, square


def share(square):
    terms = [square]
    mask = lax.axis_size("dims") // 2
    while mask >= 1:
        terms = terms + [flip(term, "dims", mask) for term in terms]
        mask //= 2
    return terms


def update_kernel(*refs, count, block):
    terms = refs[:count]
    accum_ref, table_ref, grad_ref, own_ref, other_ref = refs[count : count + 5]
    pooled_hbm, table_hbm, accum_hbm, pooled_ref, new_ref, total_ref, sems = refs[count + 5 :]
    copies = [pltpu.make_async_copy(pooled_ref, pooled_hbm, sems.at[0])]
    pooled_ref[...] = own_ref[...] + other_ref[...]
    copies[0].start()
    row_local = grad_ref.shape[1]
    for index, start in enumerate(range(0, row_local, block)):
        rows = slice(start, start + block)
        sums = [term[:, rows] for term in terms]
        while len(sums) > 1:
            half = len(sums) // 2
            sums = [sums[place] + sums[place + half] for place in range(half)]
        total = accum_ref[:, rows] + sums[0] / D
        total_ref[:, rows] = total
        scale = step_size / jnp.sqrt(total)
        new_ref[:, rows] = (
            table_ref[:, rows].astype(jnp.float32) - grad_ref[:, rows] * scale
        ).astype(jnp.bfloat16)
        copies.append(
            pltpu.make_async_copy(
                new_ref.at[:, pl.ds(start, block)], table_hbm.at[:, pl.ds(start, block)],
                sems.at[1 + index],
            )
        )
        copies[-1].start()
    copies.append(pltpu.make_async_copy(total_ref, accum_hbm, sems.at[len(copies)]))
    copies[-1].start()
    for copy in copies:
        copy.wait()


def update(table, accum, row_grad, square, sums):
    terms = share(square)
    row_local = table.shape[1]
    block = math.gcd(row_local, 1024)
    hbm = pl.BlockSpec(memory_space=pltpu.HBM)
    vmem = pl.BlockSpec(memory_space=pltpu.VMEM)
    pooled, new_table, new_accum = pl.pallas_call(
        functools.partial(update_kernel, count=len(terms), block=block),
        in_specs=[vmem] * (len(terms) + 5),
        out_specs=[hbm] * 3,
        out_shape=[
            jax.ShapeDtypeStruct(sums[0].shape, jnp.float32),
            jax.ShapeDtypeStruct(table.shape, table.dtype),
            jax.ShapeDtypeStruct((1, row_local), jnp.float32),
        ],
        scratch_shapes=[
            pltpu.VMEM(sums[0].shape, jnp.float32),
            pltpu.VMEM(table.shape, table.dtype),
            pltpu.VMEM((1, row_local), jnp.float32),
            pltpu.SemaphoreType.DMA((row_local // block + 2,)),
        ],
        compiler_params=pltpu.CompilerParams(vmem_limit_bytes=VMEM_LIMIT),
        name="update",
    )(*terms, accum[None], table, row_grad, *sums)
    return pooled[0], new_table, new_accum[0]


def fits(table, grad_pooled, peers):
    return (
        peers & (peers - 1) == 0
        and peers > 2
        and lax.axis_size("dims") & (lax.axis_size("dims") - 1) == 0
        and grad_pooled.shape[2] == LANES
        and peers * table.shape[2] * LANES * 2 <= FAST_BYTES
    )


def shards(table, accum, grad_pooled, sample_slot, row_slot, weight, send_count):
    peers = lax.axis_size("rows")
    if not fits(table, grad_pooled, peers):
        return plain(table, accum, grad_pooled, sample_slot, row_slot, weight, send_count)
    outs = []
    for feature in range(table.shape[0]):
        sums, row_grad, square = staged(
            table[feature], grad_pooled[feature], sample_slot[feature, 0],
            row_slot[feature, 0], weight[feature, 0], send_count[feature, 0],
        )
        outs.append(update(table[feature], accum[feature], row_grad, square, sums))
    return tuple(jnp.stack(out) for out in zip(*outs))


def plain(table, accum, grad_pooled, sample_slot, row_slot, weight, send_count):
    feat_count, dim_local, row_local = table.shape
    peer_count = lax.axis_size("rows")
    own_samples = grad_pooled.shape[2]
    slot_count = sample_slot.shape[3]
    entry_count = peer_count * slot_count
    block_rows = math.gcd(row_local, 512)
    block_count = row_local // block_rows
    sample_local = sample_slot.reshape(feat_count, peer_count, slot_count)
    row_index = row_slot.reshape(feat_count, peer_count, slot_count)
    flat_rows = row_index.reshape(feat_count, 1, entry_count)
    live_count = send_count.reshape(feat_count, peer_count)
    slot_iota = lax.broadcasted_iota(jnp.int32, (1, 1, slot_count), 2)
    live_mask = slot_iota < live_count[:, :, None]
    weights = jnp.where(live_mask, weight.reshape(feat_count, peer_count, slot_count), 0)
    flat_weights = weights.reshape(feat_count, 1, entry_count).astype(jnp.bfloat16)
    block_iota = lax.broadcasted_iota(jnp.int32, (1, block_rows, 1), 1)

    def lookup_block(carry, block):
        start = block * block_rows
        table_part = lax.dynamic_slice_in_dim(table, start, block_rows, 2)
        selector = (flat_rows == block_iota + start).astype(jnp.bfloat16)
        return (
            carry
            + jnp.einsum("fdr,fre->fde", table_part, selector, preferred_element_type=jnp.float32),
            None,
        )

    looked_up, _ = lax.scan(
        lookup_block,
        jnp.zeros((feat_count, dim_local, entry_count), jnp.float32),
        jnp.arange(block_count, dtype=jnp.int32),
    )
    picked = looked_up.astype(jnp.bfloat16).reshape(feat_count, dim_local, peer_count, slot_count)
    positions = lax.broadcasted_iota(jnp.int32, (1, 1, 1, own_samples), 3)
    onehot = jnp.where(sample_local[..., None] == positions, weights[..., None], 0).astype(
        jnp.bfloat16
    )
    pooled = lax.psum_scatter(
        jnp.einsum("fdnk,fnkj->nfdj", picked, onehot, preferred_element_type=jnp.float32),
        "rows",
        scatter_dimension=0,
        tiled=True,
    ).reshape(feat_count, dim_local, own_samples)
    all_grads = lax.all_gather(grad_pooled, "rows", axis=2, tiled=True)
    all_grads = all_grads.reshape(feat_count, dim_local, peer_count, own_samples)
    selector = (sample_local[..., None] == positions).astype(jnp.bfloat16)
    entry_values = jnp.einsum(
        "fdnj,fnkj->fdnk", all_grads, selector, preferred_element_type=jnp.float32
    ).astype(jnp.bfloat16)
    entry_flat = entry_values.reshape(feat_count, dim_local, entry_count)

    def gradient_block(block):
        start = block * block_rows
        weighted = jnp.where(flat_rows == block_iota + start, flat_weights, 0)
        return jnp.einsum("fde,fre->fdr", entry_flat, weighted, preferred_element_type=jnp.float32)

    grad_blocks = lax.map(gradient_block, jnp.arange(block_count, dtype=jnp.int32))
    row_grad = jnp.moveaxis(grad_blocks, 0, 2).reshape(feat_count, dim_local, row_local)
    squares = jnp.sum(row_grad * row_grad, axis=1)
    norm_total = lax.psum(squares, "dims")
    new_accum = accum + norm_total / D
    new_table = (
        table.astype(jnp.float32) - step_size * row_grad / jnp.sqrt(new_accum)[:, None, :]
    ).astype(jnp.bfloat16)
    return (pooled, new_table, new_accum)


def solution(mesh):
    return jax.shard_map(
        shards,
        mesh=mesh,
        in_specs=(
            P(None, "dims", "rows"),
            P(None, "rows"),
            P(None, "dims", "rows"),
            P(None, "rows", None, None),
            P(None, "rows", None, None),
            P(None, "rows", None, None),
            P(None, "rows", None),
        ),
        out_specs=(P(None, "dims", "rows"), P(None, "dims", "rows"), P(None, "rows")),
        check_vma=False,
    )
```

```python
import functools
import math

import jax
import jax.numpy as jnp
from jax import lax
from jax.experimental import pallas as pl
from jax.experimental.pallas import tpu as pltpu
from jax.sharding import PartitionSpec as P


D = 256


step_size = 0.3


LANES = 128
CHUNK = 256
NARROW = jnp.float8_e4m3fn
EXACT = 256.0
FAST_BYTES = 24 << 20
VMEM_LIMIT = 16 << 20


def factor_product(row, sample, weight, count, low, span, depth):
    row = row[:, :depth]
    slot = lax.broadcasted_iota(jnp.int32, row.shape, 1)
    live = jnp.where(slot < count, weight[:, :depth], 0).astype(jnp.bfloat16)
    left_key = (row % low).astype(jnp.int16)
    right_key = ((row // low) * LANES + sample[:, :depth]).astype(jnp.int16)
    left_iota = lax.broadcasted_iota(jnp.int16, (low, depth), 0)
    right_iota = lax.broadcasted_iota(jnp.int16, (span * LANES, depth), 0)
    zero = jnp.bfloat16(0)
    left = jnp.where(left_iota == left_key, live, zero).astype(NARROW)
    right = jnp.where(right_iota == right_key, jnp.bfloat16(1), zero).astype(NARROW)
    return lax.dot_general(
        left, right, (((1,), (1,)), ((), ())), preferred_element_type=jnp.float32
    )


def count_kernel(*refs, first, masks, now, low, span, chunks):
    sources = refs[:5]
    extra = 6 if first else 0
    if first:
        grad_hbm = refs[5]
        refs = refs[6:]
    else:
        refs = refs[5:]
    counts_ref, out_ref, low_ref, peak_ref = refs[:4]
    held = refs[4 : 4 + extra]
    count_ref, most_ref, spill_ref, sum_ref, sems = refs[4 + extra :]
    pooled_ref = sum_ref if first else out_ref
    loads = []
    if first:
        loads = [
            pltpu.make_async_copy(source, target, sems.at[index])
            for index, (source, target) in enumerate(zip((*sources, grad_hbm), held))
        ]
        for load in loads:
            load.start()
        _, row_ref, sample_ref, weight_ref, table_ref = held[:5]
        scalars = pltpu.make_async_copy(sources[0], count_ref, sems.at[6])
    else:
        _, row_ref, sample_ref, weight_ref, table_ref = sources
        scalars = pltpu.make_async_copy(sources[0], count_ref, sems.at[6])
    scalars.start()
    me = lax.axis_index("rows")
    most_ref[...] = jnp.zeros_like(most_ref)
    for load in loads[:4]:
        load.wait()
    scalars.wait()

    odd = lax.axis_index("dims") % 2

    def owner_of(index):
        even_mask, odd_mask = masks[0], crossed(masks[0])
        for place, mask in enumerate(masks[1:], 1):
            even_mask = jnp.where(index == place, mask, even_mask)
            odd_mask = jnp.where(index == place, crossed(mask), odd_mask)
        return me ^ jnp.where(odd == 1, odd_mask, even_mask)

    def count_pair(pair, carry):
        for member in range(2):
            owner = owner_of(2 * pair + member)
            count = count_ref[0, owner]
            row = row_ref[pl.ds(owner, 1), :]
            sample = sample_ref[pl.ds(owner, 1), :]
            weight = weight_ref[pl.ds(owner, 1), :]
            needed = jnp.maximum((count + CHUNK - 1) // CHUNK, 1)
            for chunk in range(1, chunks + 1):

                @pl.when(needed == chunk)
                def _(chunk=chunk):
                    depth = min(chunk * CHUNK, row.shape[1])
                    counts = factor_product(row, sample, weight, count, low, span, depth)
                    counts = counts.astype(jnp.bfloat16)
                    peak = most_ref[...]
                    for part in range(span):
                        piece = counts[:, part * LANES : (part + 1) * LANES]
                        counts_ref[
                            pair, part * low : (part + 1) * low,
                            member * LANES : (member + 1) * LANES,
                        ] = piece
                        peak = jnp.maximum(peak, piece)
                    most_ref[...] = peak

        if first:

            @pl.when(pair == 0)
            def _():
                for load in loads[4:]:
                    load.wait()

        @pl.when(pair < now)
        def _():
            pooled = jnp.dot(table_ref[...], counts_ref[pair], preferred_element_type=jnp.float32)
            pooled_ref[2 * pair] = pooled[:, :LANES]
            pooled_ref[2 * pair + 1] = pooled[:, LANES:]

        if now < len(masks) // 2:

            @pl.when(pair >= now)
            def _():
                pooled_ref[2 * pair] = jnp.zeros(pooled_ref.shape[1:], jnp.float32)
                pooled_ref[2 * pair + 1] = jnp.zeros(pooled_ref.shape[1:], jnp.float32)

        return carry

    lax.fori_loop(0, len(masks) // 2, count_pair, 0)

    most = most_ref[0:16, :]
    for start in range(16, low, 16):
        most = jnp.maximum(most, most_ref[start : start + 16, :])
    peak_ref[...] = most.astype(jnp.float32)

    @pl.when(jnp.max(peak_ref[...]) >= EXACT)
    def _():
        def redo(index, carry):
            owner = owner_of(index)
            counts = factor_product(
                row_ref[pl.ds(owner, 1), :], sample_ref[pl.ds(owner, 1), :],
                weight_ref[pl.ds(owner, 1), :], count_ref[0, owner], low, span, row_ref.shape[1],
            )
            rest = (counts - counts.astype(jnp.bfloat16).astype(jnp.float32)).astype(jnp.bfloat16)
            for part in range(span):
                spill_ref[part * low : (part + 1) * low, :] = rest[
                    :, part * LANES : (part + 1) * LANES
                ]
            pooled_ref[index] += jnp.dot(
                table_ref[...], spill_ref[...], preferred_element_type=jnp.float32
            )
            copy = pltpu.make_async_copy(spill_ref, low_ref.at[index], sems.at[0])
            copy.start()
            copy.wait()
            return carry

        lax.fori_loop(0, len(masks), redo, 0)

    if first:
        sums = sum_ref[...]
        head = sums.astype(jnp.bfloat16)
        out_ref[: len(masks)] = head
        out_ref[len(masks) :] = (sums - head.astype(jnp.float32)).astype(jnp.bfloat16)


def count_call(masks, now, operands, grad, peers):
    first = grad is not None
    _, row, _, _, table = operands
    total = len(masks)
    dim_local, row_local = table.shape
    slots = row.shape[1]
    low = math.gcd(row_local, 512)
    span = row_local // low
    hbm = pl.BlockSpec(memory_space=pltpu.HBM)
    vmem = pl.BlockSpec(memory_space=pltpu.VMEM)
    if first:
        arguments = [
            pltpu.with_memory_space_constraint(value, pltpu.HBM) for value in (*operands, grad)
        ]
    else:
        arguments = list(operands)
    held = [jax.ShapeDtypeStruct(value.shape, value.dtype) for value in arguments] if first else []
    return pl.pallas_call(
        functools.partial(
            count_kernel, first=first, masks=masks, now=now, low=low, span=span,
            chunks=-(-slots // CHUNK),
        ),
        in_specs=[hbm if first else vmem] * len(arguments),
        out_specs=[vmem, vmem, hbm, vmem] + [vmem] * len(held),
        scratch_shapes=[
            pltpu.SMEM((1, peers), jnp.int32),
            pltpu.VMEM((low, LANES), jnp.bfloat16),
            pltpu.VMEM((row_local, LANES), jnp.bfloat16),
            pltpu.VMEM((total, dim_local, LANES), jnp.float32),
            pltpu.SemaphoreType.DMA((7,)),
        ],
        out_shape=[
            jax.ShapeDtypeStruct((total // 2, row_local, 2 * LANES), jnp.bfloat16),
            jax.ShapeDtypeStruct((2 * total, dim_local, LANES), jnp.bfloat16)
            if first
            else jax.ShapeDtypeStruct((total, dim_local, LANES), jnp.float32),
            jax.ShapeDtypeStruct((total, row_local, LANES), jnp.bfloat16),
            jax.ShapeDtypeStruct((16, LANES), jnp.float32),
        ]
        + held,
        compiler_params=pltpu.CompilerParams(vmem_limit_bytes=VMEM_LIMIT),
        name="counts",
    )(*arguments)


def grad_kernel(*refs, terms, parts, pieces, block, chained, last, pool):
    flag_refs = refs[:parts]
    counts_refs = refs[parts : 2 * parts]
    low_refs = refs[2 * parts : 3 * parts]
    grads = refs[3 * parts : 3 * parts + pieces]
    rest = list(refs[3 * parts + pieces :])
    before_ref = rest.pop(0) if chained else None
    if pool is not None:
        table_ref, partial_ref = rest.pop(0), rest.pop(0)
    grad_ref = rest.pop(0)
    square_ref = rest.pop(0) if last else None
    if pool is not None:
        pooled_ref = rest.pop(0)
        for index, pair in enumerate(range(pool, counts_refs[1].shape[0])):
            pooled = jnp.dot(
                table_ref[...], counts_refs[1][pair], preferred_element_type=jnp.float32
            )
            for member in range(2):
                pooled_ref[2 * index + member] = (
                    partial_ref[2 * pair + member]
                    + pooled[:, member * LANES : (member + 1) * LANES]
                )
    spill_ref, sem = rest
    row_local = grad_ref.shape[1]
    lefts = [
        jnp.concatenate([grads[piece][place] for piece, place in term[2:]], axis=1)
        for term in terms
    ]
    for start in range(0, row_local, block):
        rows = slice(start, start + block)
        total = before_ref[:, rows] if chained else None
        for left, (part, pair, *_) in zip(lefts, terms):
            found = lax.dot_general(
                left, counts_refs[part][pair, rows, :], (((1,), (1,)), ((), ())),
                preferred_element_type=jnp.float32,
            )
            total = found if total is None else total + found
        grad_ref[:, rows] = total
        if last:
            square_ref[:, rows] = jnp.sum(total * total, axis=0, keepdims=True)

    for part in range(parts):
        mine = [term for term in terms if term[0] == part]
        if not mine:
            continue

        @pl.when(jnp.max(flag_refs[part][...]) >= EXACT)
        def _(part=part, mine=mine):
            for _, pair, *homes in mine:
                for member, (piece, place) in enumerate(homes):
                    copy = pltpu.make_async_copy(low_refs[part].at[2 * pair + member], spill_ref, sem)
                    copy.start()
                    copy.wait()
                    for start in range(0, row_local, block):
                        rows = slice(start, start + block)
                        grad_ref[:, rows] += lax.dot_general(
                            grads[piece][place], spill_ref[rows, :], (((1,), (1,)), ((), ())),
                            preferred_element_type=jnp.float32,
                        )
            if last:
                for start in range(0, row_local, block):
                    rows = slice(start, start + block)
                    final = grad_ref[:, rows]
                    square_ref[:, rows] = jnp.sum(final * final, axis=0, keepdims=True)


def grad_call(terms, flags, counts, lows, grads, before, last, pool=None, extra=()):
    parts = len(counts)
    row_local = counts[0].shape[1]
    dim_local = grads[0].shape[1]
    chained = before is not None
    vmem = pl.BlockSpec(memory_space=pltpu.VMEM)
    hbm = pl.BlockSpec(memory_space=pltpu.HBM)
    out = [jax.ShapeDtypeStruct((dim_local, row_local), jnp.float32)]
    if last:
        out.append(jax.ShapeDtypeStruct((1, row_local), jnp.float32))
    if pool is not None:
        late = 2 * (counts[1].shape[0] - pool)
        out.append(jax.ShapeDtypeStruct((late, dim_local, LANES), jnp.float32))
    return pl.pallas_call(
        functools.partial(
            grad_kernel, terms=terms, pool=pool, parts=parts, pieces=len(grads),
            block=math.gcd(row_local, 512), chained=chained, last=last,
        ),
        in_specs=[vmem] * parts + [vmem] * parts + [hbm] * parts + [vmem] * (len(grads) + chained + len(extra)),
        out_specs=[vmem] * len(out),
        out_shape=out,
        scratch_shapes=[pltpu.VMEM((row_local, LANES), jnp.bfloat16), pltpu.SemaphoreType.DMA],
        compiler_params=pltpu.CompilerParams(vmem_limit_bytes=VMEM_LIMIT),
        name="grads",
    )(*flags, *counts, *lows, *grads, *([before] if chained else []), *extra)


def crossed(mask):
    return (mask & ~3) | ((mask & 1) << 1) | ((mask & 2) >> 1)


def flip(value, mask):
    rows, dims = lax.axis_size("rows"), lax.axis_size("dims")
    pairs = [
        (row * dims + dim, (row ^ (crossed(mask) if dim % 2 else mask)) * dims + dim)
        for row in range(rows)
        for dim in range(dims)
    ]
    return lax.ppermute(value, ("rows", "dims"), pairs)


def flip_dims(value, mask):
    pairs = [(index, index ^ mask) for index in range(lax.axis_size("dims"))]
    return lax.ppermute(value, "dims", pairs)


def plan(peers):
    bits = [1 << place for place in range(peers.bit_length() - 1)]
    gather_bits = bits[-1:] + bits[:-1]
    stages = len(bits)
    blocks = [None] * stages
    phases = [None] * stages
    blocks[-1] = [0]
    for stage in reversed(range(stages)):
        if stage < stages - 1:
            blocks[stage] = phases[stage + 1] + blocks[stage + 1]
        phases[stage] = [bits[stage] ^ mask for mask in blocks[stage]]
    return bits, gather_bits, blocks, phases


def staged(table, grad_pooled, sample, row, weight, send_count):
    bits, gather_bits, blocks, phases = plan(lax.axis_size("rows"))
    stages = len(bits)
    passes = [phases[0], blocks[0]]
    peers = lax.axis_size("rows")
    now = len(phases[1]) // 2 if stages > 2 else len(passes[1]) // 2

    pieces = [grad_pooled[None]]
    homes = [(0, (0, 0))]

    def gathered():
        sizes = [sum(home[0] == index for _, home in homes) for index in range(len(pieces))]
        return [piece[:size] for piece, size in zip(pieces, sizes)]

    def arrived(piece, bit):
        homes.extend(
            [(mask ^ bit, (len(pieces), place)) for place, (mask, _) in enumerate(homes)]
        )
        pieces.append(piece)

    arrived(flip(pieces[0], gather_bits[0]), gather_bits[0])
    counts0, halves, low0, flag0, *held = count_call(
        passes[0], len(passes[0]) // 2, (send_count[None], row, sample, weight, table), pieces[0], peers
    )
    pieces[0] = held.pop()
    halves, pieces[1] = lax.optimization_barrier((halves, pieces[1]))
    sent = len(homes)
    message = flip(jnp.concatenate(gathered() + [halves]), bits[0])
    arrived(message, gather_bits[1])
    known = {mask for mask, _ in homes}
    counts1, partial1, low1, flag1 = count_call(passes[1], now, tuple(held), None, peers)
    partial1, message = lax.optimization_barrier((partial1, message))
    pieces[-1] = message
    half = len(passes[0])
    add = message[sent : sent + half].astype(jnp.float32) + message[sent + half :].astype(jnp.float32)
    held_back = 2 * now
    total = (partial1 + add)[:held_back]

    flags, counts, lows = [flag0, flag1], [counts0, counts1], [low0, low1]
    row_grad = None
    for stage in range(1, stages):
        take = len(phases[stage])
        if stage + 1 < stages:
            arrived(
                flip(jnp.concatenate(gathered()), gather_bits[stage + 1]),
                gather_bits[stage + 1],
            )
        incoming = flip(total[:take], bits[stage])
        total = total[take:]
        if stage == 1:
            spots = dict(homes)
            early, late = [], []
            for part, masks in enumerate(passes):
                for pair in range(len(masks) // 2):
                    two = masks[2 * pair : 2 * pair + 2]
                    (early if set(two) <= known else late).append((part, pair, two))
            if held_back < len(passes[1]):
                terms = [(part, pair, *(spots[mask] for mask in two)) for part, pair, two in early]
                used = 1 + max(home[0] for term in terms for home in term[2:])
                row_grad, rest = grad_call(
                    terms, flags, counts, lows, pieces[:used], None, False,
                    now, (held[4], partial1),
                )
                total = rest + add[held_back:]
            else:
                late = early + late
        if stage < stages - 1:
            total = total + incoming

    spots = dict(homes)
    terms = [(part, pair, *(spots[mask] for mask in two)) for part, pair, two in late]
    row_grad, square = grad_call(terms, flags, counts, lows, pieces, row_grad, True)
    return (total, incoming), row_grad, square


def share(square):
    size = lax.axis_size("dims")
    mask = 1
    while 2 * mask < size:
        square = square + flip_dims(square, mask)
        mask *= 2
    return [square, flip_dims(square, mask)] if size > 1 else [square]


def update_kernel(*refs, count, block):
    terms = refs[:count]
    accum_ref, table_ref, grad_ref, own_ref, other_ref = refs[count : count + 5]
    pooled_hbm, table_hbm, accum_hbm, pooled_ref, new_ref, total_ref, sems = refs[count + 5 :]
    copies = [pltpu.make_async_copy(pooled_ref, pooled_hbm, sems.at[0])]
    pooled_ref[...] = own_ref[...] + other_ref[...]
    copies[0].start()
    row_local = grad_ref.shape[1]
    for index, start in enumerate(range(0, row_local, block)):
        rows = slice(start, start + block)
        squares = terms[0][:, rows]
        for term in terms[1:]:
            squares = squares + term[:, rows]
        total = accum_ref[:, rows] + squares / D
        total_ref[:, rows] = total
        scale = step_size / jnp.sqrt(total)
        new_ref[:, rows] = (
            table_ref[:, rows].astype(jnp.float32) - grad_ref[:, rows] * scale
        ).astype(jnp.bfloat16)
        copies.append(
            pltpu.make_async_copy(
                new_ref.at[:, pl.ds(start, block)], table_hbm.at[:, pl.ds(start, block)],
                sems.at[1 + index],
            )
        )
        copies[-1].start()
    copies.append(pltpu.make_async_copy(total_ref, accum_hbm, sems.at[len(copies)]))
    copies[-1].start()
    for copy in copies:
        copy.wait()


def update(table, accum, row_grad, square, sums):
    terms = share(square)
    row_local = table.shape[1]
    block = math.gcd(row_local, 1024)
    hbm = pl.BlockSpec(memory_space=pltpu.HBM)
    vmem = pl.BlockSpec(memory_space=pltpu.VMEM)
    pooled, new_table, new_accum = pl.pallas_call(
        functools.partial(update_kernel, count=len(terms), block=block),
        in_specs=[vmem] * (len(terms) + 5),
        out_specs=[hbm] * 3,
        out_shape=[
            jax.ShapeDtypeStruct(sums[0].shape, jnp.float32),
            jax.ShapeDtypeStruct(table.shape, table.dtype),
            jax.ShapeDtypeStruct((1, row_local), jnp.float32),
        ],
        scratch_shapes=[
            pltpu.VMEM(sums[0].shape, jnp.float32),
            pltpu.VMEM(table.shape, table.dtype),
            pltpu.VMEM((1, row_local), jnp.float32),
            pltpu.SemaphoreType.DMA((row_local // block + 2,)),
        ],
        compiler_params=pltpu.CompilerParams(vmem_limit_bytes=VMEM_LIMIT),
        name="update",
    )(*terms, accum[None], table, row_grad, *sums)
    return pooled[0], new_table, new_accum[0]


def fits(table, grad_pooled, peers):
    return (
        peers & (peers - 1) == 0
        and peers > 2
        and lax.axis_size("dims") & (lax.axis_size("dims") - 1) == 0
        and grad_pooled.shape[2] == LANES
        and peers * table.shape[2] * LANES * 2 <= FAST_BYTES
    )


def shards(table, accum, grad_pooled, sample_slot, row_slot, weight, send_count):
    peers = lax.axis_size("rows")
    if not fits(table, grad_pooled, peers):
        return plain(table, accum, grad_pooled, sample_slot, row_slot, weight, send_count)
    outs = []
    for feature in range(table.shape[0]):
        sums, row_grad, square = staged(
            table[feature], grad_pooled[feature], sample_slot[feature, 0],
            row_slot[feature, 0], weight[feature, 0], send_count[feature, 0],
        )
        outs.append(update(table[feature], accum[feature], row_grad, square, sums))
    return tuple(jnp.stack(out) for out in zip(*outs))


def plain(table, accum, grad_pooled, sample_slot, row_slot, weight, send_count):
    feat_count, dim_local, row_local = table.shape
    peer_count = lax.axis_size("rows")
    own_samples = grad_pooled.shape[2]
    slot_count = sample_slot.shape[3]
    entry_count = peer_count * slot_count
    block_rows = math.gcd(row_local, 512)
    block_count = row_local // block_rows
    sample_local = sample_slot.reshape(feat_count, peer_count, slot_count)
    row_index = row_slot.reshape(feat_count, peer_count, slot_count)
    flat_rows = row_index.reshape(feat_count, 1, entry_count)
    live_count = send_count.reshape(feat_count, peer_count)
    slot_iota = lax.broadcasted_iota(jnp.int32, (1, 1, slot_count), 2)
    live_mask = slot_iota < live_count[:, :, None]
    weights = jnp.where(live_mask, weight.reshape(feat_count, peer_count, slot_count), 0)
    flat_weights = weights.reshape(feat_count, 1, entry_count).astype(jnp.bfloat16)
    block_iota = lax.broadcasted_iota(jnp.int32, (1, block_rows, 1), 1)

    def lookup_block(carry, block):
        start = block * block_rows
        table_part = lax.dynamic_slice_in_dim(table, start, block_rows, 2)
        selector = (flat_rows == block_iota + start).astype(jnp.bfloat16)
        return (
            carry
            + jnp.einsum("fdr,fre->fde", table_part, selector, preferred_element_type=jnp.float32),
            None,
        )

    looked_up, _ = lax.scan(
        lookup_block,
        jnp.zeros((feat_count, dim_local, entry_count), jnp.float32),
        jnp.arange(block_count, dtype=jnp.int32),
    )
    picked = looked_up.astype(jnp.bfloat16).reshape(feat_count, dim_local, peer_count, slot_count)
    positions = lax.broadcasted_iota(jnp.int32, (1, 1, 1, own_samples), 3)
    onehot = jnp.where(sample_local[..., None] == positions, weights[..., None], 0).astype(
        jnp.bfloat16
    )
    pooled = lax.psum_scatter(
        jnp.einsum("fdnk,fnkj->nfdj", picked, onehot, preferred_element_type=jnp.float32),
        "rows",
        scatter_dimension=0,
        tiled=True,
    ).reshape(feat_count, dim_local, own_samples)
    all_grads = lax.all_gather(grad_pooled, "rows", axis=2, tiled=True)
    all_grads = all_grads.reshape(feat_count, dim_local, peer_count, own_samples)
    selector = (sample_local[..., None] == positions).astype(jnp.bfloat16)
    entry_values = jnp.einsum(
        "fdnj,fnkj->fdnk", all_grads, selector, preferred_element_type=jnp.float32
    ).astype(jnp.bfloat16)
    entry_flat = entry_values.reshape(feat_count, dim_local, entry_count)

    def gradient_block(block):
        start = block * block_rows
        weighted = jnp.where(flat_rows == block_iota + start, flat_weights, 0)
        return jnp.einsum("fde,fre->fdr", entry_flat, weighted, preferred_element_type=jnp.float32)

    grad_blocks = lax.map(gradient_block, jnp.arange(block_count, dtype=jnp.int32))
    row_grad = jnp.moveaxis(grad_blocks, 0, 2).reshape(feat_count, dim_local, row_local)
    squares = jnp.sum(row_grad * row_grad, axis=1)
    norm_total = lax.psum(squares, "dims")
    new_accum = accum + norm_total / D
    new_table = (
        table.astype(jnp.float32) - step_size * row_grad / jnp.sqrt(new_accum)[:, None, :]
    ).astype(jnp.bfloat16)
    return (pooled, new_table, new_accum)


def solution(mesh):
    return jax.shard_map(
        shards,
        mesh=mesh,
        in_specs=(
            P(None, "dims", "rows"),
            P(None, "rows"),
            P(None, "dims", "rows"),
            P(None, "rows", None, None),
            P(None, "rows", None, None),
            P(None, "rows", None, None),
            P(None, "rows", None),
        ),
        out_specs=(P(None, "dims", "rows"), P(None, "dims", "rows"), P(None, "rows")),
        check_vma=False,
    )
```

```python
import functools
import math

import jax
import jax.numpy as jnp
from jax import lax
from jax.experimental import pallas as pl
from jax.experimental.pallas import tpu as pltpu
from jax.sharding import PartitionSpec as P


D = 256


step_size = 0.3


LANES = 128
CHUNK = 256
NARROW = jnp.float8_e4m3fn
EXACT = 256.0
FAST_BYTES = 24 << 20
VMEM_LIMIT = 16 << 20


def factor_product(row, sample, weight, count, low, span, depth):
    row = row[:, :depth]
    slot = lax.broadcasted_iota(jnp.int32, row.shape, 1)
    live = jnp.where(slot < count, weight[:, :depth], 0).astype(jnp.bfloat16)
    left_key = (row % low).astype(jnp.int16)
    right_key = ((row // low) * LANES + sample[:, :depth]).astype(jnp.int16)
    left_iota = lax.broadcasted_iota(jnp.int16, (low, depth), 0)
    right_iota = lax.broadcasted_iota(jnp.int16, (span * LANES, depth), 0)
    zero = jnp.bfloat16(0)
    left = jnp.where(left_iota == left_key, live, zero).astype(NARROW)
    right = jnp.where(right_iota == right_key, jnp.bfloat16(1), zero).astype(NARROW)
    return lax.dot_general(
        left, right, (((1,), (1,)), ((), ())), preferred_element_type=jnp.float32
    )


def count_kernel(*refs, first, masks, now, low, span, chunks):
    sources = refs[:5]
    extra = 6 if first else 0
    if first:
        grad_hbm = refs[5]
        refs = refs[6:]
    else:
        refs = refs[5:]
    counts_ref, out_ref, low_ref, peak_ref = refs[:4]
    held = refs[4 : 4 + extra]
    count_ref, most_ref, spill_ref, sum_ref, sems = refs[4 + extra :]
    pooled_ref = sum_ref if first else out_ref
    loads = []
    if first:
        loads = [
            pltpu.make_async_copy(source, target, sems.at[index])
            for index, (source, target) in enumerate(zip((*sources, grad_hbm), held))
        ]
        for load in loads:
            load.start()
        _, row_ref, sample_ref, weight_ref, table_ref = held[:5]
        scalars = pltpu.make_async_copy(sources[0], count_ref, sems.at[6])
    else:
        _, row_ref, sample_ref, weight_ref, table_ref = sources
        scalars = pltpu.make_async_copy(sources[0], count_ref, sems.at[6])
    scalars.start()
    me = lax.axis_index("rows")
    most_ref[...] = jnp.zeros_like(most_ref)
    for load in loads[:4]:
        load.wait()
    scalars.wait()

    odd = lax.axis_index("dims") % 2

    def owner_of(index):
        even_mask, odd_mask = masks[0], crossed(masks[0])
        for place, mask in enumerate(masks[1:], 1):
            even_mask = jnp.where(index == place, mask, even_mask)
            odd_mask = jnp.where(index == place, crossed(mask), odd_mask)
        return me ^ jnp.where(odd == 1, odd_mask, even_mask)

    def count_pair(pair, carry):
        for member in range(2):
            owner = owner_of(2 * pair + member)
            count = count_ref[0, owner]
            row = row_ref[pl.ds(owner, 1), :]
            sample = sample_ref[pl.ds(owner, 1), :]
            weight = weight_ref[pl.ds(owner, 1), :]
            needed = jnp.maximum((count + CHUNK - 1) // CHUNK, 1)
            for chunk in range(1, chunks + 1):

                @pl.when(needed == chunk)
                def _(chunk=chunk):
                    depth = min(chunk * CHUNK, row.shape[1])
                    counts = factor_product(row, sample, weight, count, low, span, depth)
                    counts = counts.astype(jnp.bfloat16)
                    peak = most_ref[...]
                    for part in range(span):
                        piece = counts[:, part * LANES : (part + 1) * LANES]
                        counts_ref[
                            pair, part * low : (part + 1) * low,
                            member * LANES : (member + 1) * LANES,
                        ] = piece
                        peak = jnp.maximum(peak, piece)
                    most_ref[...] = peak

        if first:

            @pl.when(pair == 0)
            def _():
                for load in loads[4:]:
                    load.wait()

        @pl.when(pair < now)
        def _():
            pooled = jnp.dot(table_ref[...], counts_ref[pair], preferred_element_type=jnp.float32)
            pooled_ref[2 * pair] = pooled[:, :LANES]
            pooled_ref[2 * pair + 1] = pooled[:, LANES:]

        if now < len(masks) // 2:

            @pl.when(pair >= now)
            def _():
                pooled_ref[2 * pair] = jnp.zeros(pooled_ref.shape[1:], jnp.float32)
                pooled_ref[2 * pair + 1] = jnp.zeros(pooled_ref.shape[1:], jnp.float32)

        return carry

    lax.fori_loop(0, len(masks) // 2, count_pair, 0)

    most = most_ref[0:16, :]
    for start in range(16, low, 16):
        most = jnp.maximum(most, most_ref[start : start + 16, :])
    peak_ref[...] = most.astype(jnp.float32)

    @pl.when(jnp.max(peak_ref[...]) >= EXACT)
    def _():
        def redo(index, carry):
            owner = owner_of(index)
            counts = factor_product(
                row_ref[pl.ds(owner, 1), :], sample_ref[pl.ds(owner, 1), :],
                weight_ref[pl.ds(owner, 1), :], count_ref[0, owner], low, span, row_ref.shape[1],
            )
            rest = (counts - counts.astype(jnp.bfloat16).astype(jnp.float32)).astype(jnp.bfloat16)
            for part in range(span):
                spill_ref[part * low : (part + 1) * low, :] = rest[
                    :, part * LANES : (part + 1) * LANES
                ]
            pooled_ref[index] += jnp.dot(
                table_ref[...], spill_ref[...], preferred_element_type=jnp.float32
            )
            copy = pltpu.make_async_copy(spill_ref, low_ref.at[index], sems.at[0])
            copy.start()
            copy.wait()
            return carry

        lax.fori_loop(0, len(masks), redo, 0)

    if first:
        sums = sum_ref[...]
        head = sums.astype(jnp.bfloat16)
        out_ref[: len(masks)] = head
        out_ref[len(masks) :] = (sums - head.astype(jnp.float32)).astype(jnp.bfloat16)


def count_call(masks, now, operands, grad, peers):
    first = grad is not None
    _, row, _, _, table = operands
    total = len(masks)
    dim_local, row_local = table.shape
    slots = row.shape[1]
    low = math.gcd(row_local, 512)
    span = row_local // low
    hbm = pl.BlockSpec(memory_space=pltpu.HBM)
    vmem = pl.BlockSpec(memory_space=pltpu.VMEM)
    if first:
        arguments = [
            pltpu.with_memory_space_constraint(value, pltpu.HBM) for value in (*operands, grad)
        ]
    else:
        arguments = list(operands)
    held = [jax.ShapeDtypeStruct(value.shape, value.dtype) for value in arguments] if first else []
    return pl.pallas_call(
        functools.partial(
            count_kernel, first=first, masks=masks, now=now, low=low, span=span,
            chunks=-(-slots // CHUNK),
        ),
        in_specs=[hbm if first else vmem] * len(arguments),
        out_specs=[vmem, vmem, hbm, vmem] + [vmem] * len(held),
        scratch_shapes=[
            pltpu.SMEM((1, peers), jnp.int32),
            pltpu.VMEM((low, LANES), jnp.bfloat16),
            pltpu.VMEM((row_local, LANES), jnp.bfloat16),
            pltpu.VMEM((total, dim_local, LANES), jnp.float32),
            pltpu.SemaphoreType.DMA((7,)),
        ],
        out_shape=[
            jax.ShapeDtypeStruct((total // 2, row_local, 2 * LANES), jnp.bfloat16),
            jax.ShapeDtypeStruct((2 * total, dim_local, LANES), jnp.bfloat16)
            if first
            else jax.ShapeDtypeStruct((total, dim_local, LANES), jnp.float32),
            jax.ShapeDtypeStruct((total, row_local, LANES), jnp.bfloat16),
            jax.ShapeDtypeStruct((16, LANES), jnp.float32),
        ]
        + held,
        compiler_params=pltpu.CompilerParams(vmem_limit_bytes=VMEM_LIMIT),
        name="counts",
    )(*arguments)


def grad_kernel(*refs, terms, parts, pieces, block, chained, last, pool):
    flag_refs = refs[:parts]
    counts_refs = refs[parts : 2 * parts]
    low_refs = refs[2 * parts : 3 * parts]
    grads = refs[3 * parts : 3 * parts + pieces]
    rest = list(refs[3 * parts + pieces :])
    before_ref = rest.pop(0) if chained else None
    if pool is not None:
        table_ref, partial_ref = rest.pop(0), rest.pop(0)
    grad_ref = rest.pop(0)
    square_ref = rest.pop(0) if last else None
    if pool is not None:
        pooled_ref = rest.pop(0)
        for index, pair in enumerate(range(pool, counts_refs[1].shape[0])):
            pooled = jnp.dot(
                table_ref[...], counts_refs[1][pair], preferred_element_type=jnp.float32
            )
            for member in range(2):
                pooled_ref[2 * index + member] = (
                    partial_ref[2 * pair + member]
                    + pooled[:, member * LANES : (member + 1) * LANES]
                )
    spill_ref, sem = rest
    row_local = grad_ref.shape[1]
    lefts = [
        jnp.concatenate([grads[piece][place] for piece, place in term[2:]], axis=1)
        for term in terms
    ]
    for start in range(0, row_local, block):
        rows = slice(start, start + block)
        total = before_ref[:, rows] if chained else None
        for left, (part, pair, *_) in zip(lefts, terms):
            found = lax.dot_general(
                left, counts_refs[part][pair, rows, :], (((1,), (1,)), ((), ())),
                preferred_element_type=jnp.float32,
            )
            total = found if total is None else total + found
        grad_ref[:, rows] = total
        if last:
            square_ref[:, rows] = jnp.sum(total * total, axis=0, keepdims=True)

    for part in range(parts):
        mine = [term for term in terms if term[0] == part]
        if not mine:
            continue

        @pl.when(jnp.max(flag_refs[part][...]) >= EXACT)
        def _(part=part, mine=mine):
            for _, pair, *homes in mine:
                for member, (piece, place) in enumerate(homes):
                    copy = pltpu.make_async_copy(low_refs[part].at[2 * pair + member], spill_ref, sem)
                    copy.start()
                    copy.wait()
                    for start in range(0, row_local, block):
                        rows = slice(start, start + block)
                        grad_ref[:, rows] += lax.dot_general(
                            grads[piece][place], spill_ref[rows, :], (((1,), (1,)), ((), ())),
                            preferred_element_type=jnp.float32,
                        )
            if last:
                for start in range(0, row_local, block):
                    rows = slice(start, start + block)
                    final = grad_ref[:, rows]
                    square_ref[:, rows] = jnp.sum(final * final, axis=0, keepdims=True)


def grad_call(terms, flags, counts, lows, grads, before, last, pool=None, extra=()):
    parts = len(counts)
    row_local = counts[0].shape[1]
    dim_local = grads[0].shape[1]
    chained = before is not None
    vmem = pl.BlockSpec(memory_space=pltpu.VMEM)
    hbm = pl.BlockSpec(memory_space=pltpu.HBM)
    out = [jax.ShapeDtypeStruct((dim_local, row_local), jnp.float32)]
    if last:
        out.append(jax.ShapeDtypeStruct((1, row_local), jnp.float32))
    if pool is not None:
        late = 2 * (counts[1].shape[0] - pool)
        out.append(jax.ShapeDtypeStruct((late, dim_local, LANES), jnp.float32))
    return pl.pallas_call(
        functools.partial(
            grad_kernel, terms=terms, pool=pool, parts=parts, pieces=len(grads),
            block=math.gcd(row_local, 512), chained=chained, last=last,
        ),
        in_specs=[vmem] * parts + [vmem] * parts + [hbm] * parts + [vmem] * (len(grads) + chained + len(extra)),
        out_specs=[vmem] * len(out),
        out_shape=out,
        scratch_shapes=[pltpu.VMEM((row_local, LANES), jnp.bfloat16), pltpu.SemaphoreType.DMA],
        compiler_params=pltpu.CompilerParams(vmem_limit_bytes=VMEM_LIMIT),
        name="grads",
    )(*flags, *counts, *lows, *grads, *([before] if chained else []), *extra)


def crossed(mask):
    return (mask & ~3) | ((mask & 1) << 1) | ((mask & 2) >> 1)


def flip(value, mask):
    rows, dims = lax.axis_size("rows"), lax.axis_size("dims")
    pairs = [
        (row * dims + dim, (row ^ (crossed(mask) if dim % 2 else mask)) * dims + dim)
        for row in range(rows)
        for dim in range(dims)
    ]
    return lax.ppermute(value, ("rows", "dims"), pairs)


def flip_dims(value, mask):
    pairs = [(index, index ^ mask) for index in range(lax.axis_size("dims"))]
    return lax.ppermute(value, "dims", pairs)


def plan(peers):
    bits = [1 << place for place in range(peers.bit_length() - 1)]
    gather_bits = bits[-1:] + bits[:-1]
    stages = len(bits)
    blocks = [None] * stages
    phases = [None] * stages
    blocks[-1] = [0]
    for stage in reversed(range(stages)):
        if stage < stages - 1:
            blocks[stage] = phases[stage + 1] + blocks[stage + 1]
        phases[stage] = [bits[stage] ^ mask for mask in blocks[stage]]
    return bits, gather_bits, blocks, phases


def staged(table, grad_pooled, sample, row, weight, send_count):
    bits, gather_bits, blocks, phases = plan(lax.axis_size("rows"))
    stages = len(bits)
    passes = [phases[0], blocks[0]]
    peers = lax.axis_size("rows")
    now = len(phases[1]) // 2 if stages > 2 else len(passes[1]) // 2

    pieces = [grad_pooled[None]]
    homes = [(0, (0, 0))]

    def gathered():
        sizes = [sum(home[0] == index for _, home in homes) for index in range(len(pieces))]
        return [piece[:size] for piece, size in zip(pieces, sizes)]

    def arrived(piece, bit):
        homes.extend(
            [(mask ^ bit, (len(pieces), place)) for place, (mask, _) in enumerate(homes)]
        )
        pieces.append(piece)

    arrived(flip(pieces[0], gather_bits[0]), gather_bits[0])
    counts0, halves, low0, flag0, *held = count_call(
        passes[0], len(passes[0]) // 2, (send_count[None], row, sample, weight, table), pieces[0], peers
    )
    pieces[0] = held.pop()
    halves, pieces[1] = lax.optimization_barrier((halves, pieces[1]))
    sent = len(homes)
    message = flip(jnp.concatenate(gathered() + [halves]), bits[0])
    arrived(message, gather_bits[1])
    known = {mask for mask, _ in homes}
    counts1, partial1, low1, flag1 = count_call(passes[1], now, tuple(held), None, peers)
    partial1, message = lax.optimization_barrier((partial1, message))
    pieces[-1] = message
    half = len(passes[0])
    add = message[sent : sent + half].astype(jnp.float32) + message[sent + half :].astype(jnp.float32)
    held_back = 2 * now
    total = (partial1 + add)[:held_back]

    flags, counts, lows = [flag0, flag1], [counts0, counts1], [low0, low1]
    row_grad = None
    for stage in range(1, stages):
        take = len(phases[stage])
        if stage + 1 < stages:
            arrived(
                flip(jnp.concatenate(gathered()), gather_bits[stage + 1]),
                gather_bits[stage + 1],
            )
        incoming = flip(total[:take], bits[stage])
        total = total[take:]
        if stage == 1:
            spots = dict(homes)
            early, late = [], []
            for part, masks in enumerate(passes):
                for pair in range(len(masks) // 2):
                    two = masks[2 * pair : 2 * pair + 2]
                    (early if set(two) <= known else late).append((part, pair, two))
            if held_back < len(passes[1]):
                terms = [(part, pair, *(spots[mask] for mask in two)) for part, pair, two in early]
                used = 1 + max(home[0] for term in terms for home in term[2:])
                row_grad, rest = grad_call(
                    terms, flags, counts, lows, pieces[:used], None, False,
                    now, (held[4], partial1),
                )
                total = rest + add[held_back:]
            else:
                late = early + late
        if stage < stages - 1:
            total = total + incoming

    spots = dict(homes)
    terms = [(part, pair, *(spots[mask] for mask in two)) for part, pair, two in late]
    row_grad, square = grad_call(terms, flags, counts, lows, pieces, row_grad, True)
    return (total, incoming), row_grad, square


def share(square):
    terms = [square]
    mask = lax.axis_size("dims") // 2
    while mask >= 1:
        terms = terms + [flip_dims(term, mask) for term in terms]
        mask //= 2
    return terms


def update_kernel(*refs, count, block):
    terms = refs[:count]
    accum_ref, table_ref, grad_ref, own_ref, other_ref = refs[count : count + 5]
    pooled_hbm, table_hbm, accum_hbm, pooled_ref, new_ref, total_ref, sems = refs[count + 5 :]
    copies = [pltpu.make_async_copy(pooled_ref, pooled_hbm, sems.at[0])]
    pooled_ref[...] = own_ref[...] + other_ref[...]
    copies[0].start()
    row_local = grad_ref.shape[1]
    for index, start in enumerate(range(0, row_local, block)):
        rows = slice(start, start + block)
        sums = [term[:, rows] for term in terms]
        while len(sums) > 1:
            half = len(sums) // 2
            sums = [sums[place] + sums[place + half] for place in range(half)]
        squares = sums[0]
        total = accum_ref[:, rows] + squares / D
        total_ref[:, rows] = total
        scale = step_size / jnp.sqrt(total)
        new_ref[:, rows] = (
            table_ref[:, rows].astype(jnp.float32) - grad_ref[:, rows] * scale
        ).astype(jnp.bfloat16)
        copies.append(
            pltpu.make_async_copy(
                new_ref.at[:, pl.ds(start, block)], table_hbm.at[:, pl.ds(start, block)],
                sems.at[1 + index],
            )
        )
        copies[-1].start()
    copies.append(pltpu.make_async_copy(total_ref, accum_hbm, sems.at[len(copies)]))
    copies[-1].start()
    for copy in copies:
        copy.wait()


def update(table, accum, row_grad, square, sums):
    terms = share(square)
    row_local = table.shape[1]
    block = math.gcd(row_local, 1024)
    hbm = pl.BlockSpec(memory_space=pltpu.HBM)
    vmem = pl.BlockSpec(memory_space=pltpu.VMEM)
    pooled, new_table, new_accum = pl.pallas_call(
        functools.partial(update_kernel, count=len(terms), block=block),
        in_specs=[vmem] * (len(terms) + 5),
        out_specs=[hbm] * 3,
        out_shape=[
            jax.ShapeDtypeStruct(sums[0].shape, jnp.float32),
            jax.ShapeDtypeStruct(table.shape, table.dtype),
            jax.ShapeDtypeStruct((1, row_local), jnp.float32),
        ],
        scratch_shapes=[
            pltpu.VMEM(sums[0].shape, jnp.float32),
            pltpu.VMEM(table.shape, table.dtype),
            pltpu.VMEM((1, row_local), jnp.float32),
            pltpu.SemaphoreType.DMA((row_local // block + 2,)),
        ],
        compiler_params=pltpu.CompilerParams(vmem_limit_bytes=VMEM_LIMIT),
        name="update",
    )(*terms, accum[None], table, row_grad, *sums)
    return pooled[0], new_table, new_accum[0]


def fits(table, grad_pooled, peers):
    return (
        peers & (peers - 1) == 0
        and peers > 2
        and lax.axis_size("dims") & (lax.axis_size("dims") - 1) == 0
        and grad_pooled.shape[2] == LANES
        and peers * table.shape[2] * LANES * 2 <= FAST_BYTES
    )


def shards(table, accum, grad_pooled, sample_slot, row_slot, weight, send_count):
    peers = lax.axis_size("rows")
    if not fits(table, grad_pooled, peers):
        return plain(table, accum, grad_pooled, sample_slot, row_slot, weight, send_count)
    outs = []
    for feature in range(table.shape[0]):
        sums, row_grad, square = staged(
            table[feature], grad_pooled[feature], sample_slot[feature, 0],
            row_slot[feature, 0], weight[feature, 0], send_count[feature, 0],
        )
        outs.append(update(table[feature], accum[feature], row_grad, square, sums))
    return tuple(jnp.stack(out) for out in zip(*outs))


def plain(table, accum, grad_pooled, sample_slot, row_slot, weight, send_count):
    feat_count, dim_local, row_local = table.shape
    peer_count = lax.axis_size("rows")
    own_samples = grad_pooled.shape[2]
    slot_count = sample_slot.shape[3]
    entry_count = peer_count * slot_count
    block_rows = math.gcd(row_local, 512)
    block_count = row_local // block_rows
    sample_local = sample_slot.reshape(feat_count, peer_count, slot_count)
    row_index = row_slot.reshape(feat_count, peer_count, slot_count)
    flat_rows = row_index.reshape(feat_count, 1, entry_count)
    live_count = send_count.reshape(feat_count, peer_count)
    slot_iota = lax.broadcasted_iota(jnp.int32, (1, 1, slot_count), 2)
    live_mask = slot_iota < live_count[:, :, None]
    weights = jnp.where(live_mask, weight.reshape(feat_count, peer_count, slot_count), 0)
    flat_weights = weights.reshape(feat_count, 1, entry_count).astype(jnp.bfloat16)
    block_iota = lax.broadcasted_iota(jnp.int32, (1, block_rows, 1), 1)

    def lookup_block(carry, block):
        start = block * block_rows
        table_part = lax.dynamic_slice_in_dim(table, start, block_rows, 2)
        selector = (flat_rows == block_iota + start).astype(jnp.bfloat16)
        return (
            carry
            + jnp.einsum("fdr,fre->fde", table_part, selector, preferred_element_type=jnp.float32),
            None,
        )

    looked_up, _ = lax.scan(
        lookup_block,
        jnp.zeros((feat_count, dim_local, entry_count), jnp.float32),
        jnp.arange(block_count, dtype=jnp.int32),
    )
    picked = looked_up.astype(jnp.bfloat16).reshape(feat_count, dim_local, peer_count, slot_count)
    positions = lax.broadcasted_iota(jnp.int32, (1, 1, 1, own_samples), 3)
    onehot = jnp.where(sample_local[..., None] == positions, weights[..., None], 0).astype(
        jnp.bfloat16
    )
    pooled = lax.psum_scatter(
        jnp.einsum("fdnk,fnkj->nfdj", picked, onehot, preferred_element_type=jnp.float32),
        "rows",
        scatter_dimension=0,
        tiled=True,
    ).reshape(feat_count, dim_local, own_samples)
    all_grads = lax.all_gather(grad_pooled, "rows", axis=2, tiled=True)
    all_grads = all_grads.reshape(feat_count, dim_local, peer_count, own_samples)
    selector = (sample_local[..., None] == positions).astype(jnp.bfloat16)
    entry_values = jnp.einsum(
        "fdnj,fnkj->fdnk", all_grads, selector, preferred_element_type=jnp.float32
    ).astype(jnp.bfloat16)
    entry_flat = entry_values.reshape(feat_count, dim_local, entry_count)

    def gradient_block(block):
        start = block * block_rows
        weighted = jnp.where(flat_rows == block_iota + start, flat_weights, 0)
        return jnp.einsum("fde,fre->fdr", entry_flat, weighted, preferred_element_type=jnp.float32)

    grad_blocks = lax.map(gradient_block, jnp.arange(block_count, dtype=jnp.int32))
    row_grad = jnp.moveaxis(grad_blocks, 0, 2).reshape(feat_count, dim_local, row_local)
    squares = jnp.sum(row_grad * row_grad, axis=1)
    norm_total = lax.psum(squares, "dims")
    new_accum = accum + norm_total / D
    new_table = (
        table.astype(jnp.float32) - step_size * row_grad / jnp.sqrt(new_accum)[:, None, :]
    ).astype(jnp.bfloat16)
    return (pooled, new_table, new_accum)


def solution(mesh):
    return jax.shard_map(
        shards,
        mesh=mesh,
        in_specs=(
            P(None, "dims", "rows"),
            P(None, "rows"),
            P(None, "dims", "rows"),
            P(None, "rows", None, None),
            P(None, "rows", None, None),
            P(None, "rows", None, None),
            P(None, "rows", None),
        ),
        out_specs=(P(None, "dims", "rows"), P(None, "dims", "rows"), P(None, "rows")),
        check_vma=False,
    )
```

```python
import functools
import math

import jax
import jax.numpy as jnp
from jax import lax
from jax.experimental import pallas as pl
from jax.experimental.pallas import tpu as pltpu
from jax.sharding import PartitionSpec as P


D = 256


step_size = 0.3


LANES = 128
CHUNK = 256
NARROW = jnp.float8_e4m3fn
EXACT = 256.0
FAST_BYTES = 24 << 20
VMEM_LIMIT = 16 << 20


def factor_product(row, sample, weight, count, low, span, depth):
    row = row[:, :depth]
    slot = lax.broadcasted_iota(jnp.int32, row.shape, 1)
    live = jnp.where(slot < count, weight[:, :depth], 0).astype(jnp.bfloat16)
    left_key = (row % low).astype(jnp.int16)
    right_key = ((row // low) * LANES + sample[:, :depth]).astype(jnp.int16)
    left_iota = lax.broadcasted_iota(jnp.int16, (low, depth), 0)
    right_iota = lax.broadcasted_iota(jnp.int16, (span * LANES, depth), 0)
    zero = jnp.bfloat16(0)
    left = jnp.where(left_iota == left_key, live, zero).astype(NARROW)
    right = jnp.where(right_iota == right_key, jnp.bfloat16(1), zero).astype(NARROW)
    return lax.dot_general(
        left, right, (((1,), (1,)), ((), ())), preferred_element_type=jnp.float32
    )


def count_kernel(*refs, first, masks, now, low, span, chunks):
    sources = refs[:5]
    extra = 6 if first else 0
    if first:
        grad_hbm = refs[5]
        refs = refs[6:]
    else:
        refs = refs[5:]
    counts_ref, out_ref, low_ref, peak_ref = refs[:4]
    held = refs[4 : 4 + extra]
    count_ref, most_ref, spill_ref, sum_ref, sems = refs[4 + extra :]
    pooled_ref = sum_ref if first else out_ref
    loads = []
    if first:
        loads = [
            pltpu.make_async_copy(source, target, sems.at[index])
            for index, (source, target) in enumerate(zip((*sources, grad_hbm), held))
        ]
        for load in loads:
            load.start()
        live_ref, row_ref, sample_ref, weight_ref, table_ref = held[:5]
    else:
        live_ref, row_ref, sample_ref, weight_ref, table_ref = sources
    me = lax.axis_index("rows")
    most_ref[...] = jnp.zeros_like(most_ref)
    for load in loads[:4]:
        load.wait()

    odd = lax.axis_index("dims") % 2

    def owner_of(index):
        even_mask, odd_mask = masks[0], crossed(masks[0])
        for place, mask in enumerate(masks[1:], 1):
            even_mask = jnp.where(index == place, mask, even_mask)
            odd_mask = jnp.where(index == place, crossed(mask), odd_mask)
        return me ^ jnp.where(odd == 1, odd_mask, even_mask)

    lives = live_ref[...].astype(jnp.float32)
    places = lax.broadcasted_iota(jnp.int32, lives.shape, 1)
    for index in range(len(masks)):
        mine = jnp.where(places == owner_of(index), lives, 0.0)
        count_ref[0, index] = jnp.sum(mine).astype(jnp.int32)

    def count_pair(pair, carry):
        for member in range(2):
            owner = owner_of(2 * pair + member)
            count = count_ref[0, 2 * pair + member]
            row = row_ref[pl.ds(owner, 1), :]
            sample = sample_ref[pl.ds(owner, 1), :]
            weight = weight_ref[pl.ds(owner, 1), :]
            needed = jnp.maximum((count + CHUNK - 1) // CHUNK, 1)
            for chunk in range(1, chunks + 1):

                @pl.when(needed == chunk)
                def _(chunk=chunk):
                    depth = min(chunk * CHUNK, row.shape[1])
                    counts = factor_product(row, sample, weight, count, low, span, depth)
                    counts = counts.astype(jnp.bfloat16)
                    peak = most_ref[...]
                    for part in range(span):
                        piece = counts[:, part * LANES : (part + 1) * LANES]
                        counts_ref[
                            pair, part * low : (part + 1) * low,
                            member * LANES : (member + 1) * LANES,
                        ] = piece
                        peak = jnp.maximum(peak, piece)
                    most_ref[...] = peak

        if first:

            @pl.when(pair == 0)
            def _():
                for load in loads[4:]:
                    load.wait()

        @pl.when(pair < now)
        def _():
            pooled = jnp.dot(table_ref[...], counts_ref[pair], preferred_element_type=jnp.float32)
            pooled_ref[2 * pair] = pooled[:, :LANES]
            pooled_ref[2 * pair + 1] = pooled[:, LANES:]

        if now < len(masks) // 2:

            @pl.when(pair >= now)
            def _():
                pooled_ref[2 * pair] = jnp.zeros(pooled_ref.shape[1:], jnp.float32)
                pooled_ref[2 * pair + 1] = jnp.zeros(pooled_ref.shape[1:], jnp.float32)

        return carry

    lax.fori_loop(0, len(masks) // 2, count_pair, 0, unroll=True)

    most = most_ref[0:16, :]
    for start in range(16, low, 16):
        most = jnp.maximum(most, most_ref[start : start + 16, :])
    peak_ref[...] = most.astype(jnp.float32)

    @pl.when(jnp.max(peak_ref[...]) >= EXACT)
    def _():
        def redo(index, carry):
            owner = owner_of(index)
            counts = factor_product(
                row_ref[pl.ds(owner, 1), :], sample_ref[pl.ds(owner, 1), :],
                weight_ref[pl.ds(owner, 1), :], count_ref[0, index], low, span, row_ref.shape[1],
            )
            rest = (counts - counts.astype(jnp.bfloat16).astype(jnp.float32)).astype(jnp.bfloat16)
            for part in range(span):
                spill_ref[part * low : (part + 1) * low, :] = rest[
                    :, part * LANES : (part + 1) * LANES
                ]
            pooled_ref[index] += jnp.dot(
                table_ref[...], spill_ref[...], preferred_element_type=jnp.float32
            )
            copy = pltpu.make_async_copy(spill_ref, low_ref.at[index], sems.at[0])
            copy.start()
            copy.wait()
            return carry

        lax.fori_loop(0, len(masks), redo, 0)

    if first:
        sums = sum_ref[...]
        head = sums.astype(jnp.bfloat16)
        out_ref[: len(masks)] = head
        out_ref[len(masks) :] = (sums - head.astype(jnp.float32)).astype(jnp.bfloat16)


def count_call(masks, now, operands, grad, peers):
    first = grad is not None
    _, row, _, _, table = operands
    total = len(masks)
    dim_local, row_local = table.shape
    slots = row.shape[1]
    low = math.gcd(row_local, 512)
    span = row_local // low
    hbm = pl.BlockSpec(memory_space=pltpu.HBM)
    vmem = pl.BlockSpec(memory_space=pltpu.VMEM)
    if first:
        arguments = [
            pltpu.with_memory_space_constraint(value, pltpu.HBM) for value in (*operands, grad)
        ]
    else:
        arguments = list(operands)
    held = [jax.ShapeDtypeStruct(value.shape, value.dtype) for value in arguments] if first else []
    return pl.pallas_call(
        functools.partial(
            count_kernel, first=first, masks=masks, now=now, low=low, span=span,
            chunks=-(-slots // CHUNK),
        ),
        in_specs=[hbm if first else vmem] * len(arguments),
        out_specs=[vmem, vmem, hbm, vmem] + [vmem] * len(held),
        scratch_shapes=[
            pltpu.SMEM((1, peers), jnp.int32),
            pltpu.VMEM((low, LANES), jnp.bfloat16),
            pltpu.VMEM((row_local, LANES), jnp.bfloat16),
            pltpu.VMEM((total, dim_local, LANES), jnp.float32),
            pltpu.SemaphoreType.DMA((6,)),
        ],
        out_shape=[
            jax.ShapeDtypeStruct((total // 2, row_local, 2 * LANES), jnp.bfloat16),
            jax.ShapeDtypeStruct((2 * total, dim_local, LANES), jnp.bfloat16)
            if first
            else jax.ShapeDtypeStruct((total, dim_local, LANES), jnp.float32),
            jax.ShapeDtypeStruct((total, row_local, LANES), jnp.bfloat16),
            jax.ShapeDtypeStruct((16, LANES), jnp.float32),
        ]
        + held,
        compiler_params=pltpu.CompilerParams(vmem_limit_bytes=VMEM_LIMIT),
        name="counts",
    )(*arguments)


def grad_kernel(*refs, terms, parts, pieces, block, chained, last, pool):
    flag_refs = refs[:parts]
    counts_refs = refs[parts : 2 * parts]
    low_refs = refs[2 * parts : 3 * parts]
    grads = refs[3 * parts : 3 * parts + pieces]
    rest = list(refs[3 * parts + pieces :])
    before_ref = rest.pop(0) if chained else None
    if pool is not None:
        table_ref, partial_ref = rest.pop(0), rest.pop(0)
    grad_ref = rest.pop(0)
    square_ref = rest.pop(0) if last else None
    if pool is not None:
        pooled_ref = rest.pop(0)
        for index, pair in enumerate(range(pool, counts_refs[1].shape[0])):
            pooled = jnp.dot(
                table_ref[...], counts_refs[1][pair], preferred_element_type=jnp.float32
            )
            for member in range(2):
                pooled_ref[2 * index + member] = (
                    partial_ref[2 * pair + member]
                    + pooled[:, member * LANES : (member + 1) * LANES]
                )
    spill_ref, sem = rest
    row_local = grad_ref.shape[1]
    lefts = [
        jnp.concatenate([grads[piece][place] for piece, place in term[2:]], axis=1)
        for term in terms
    ]
    for start in range(0, row_local, block):
        rows = slice(start, start + block)
        total = before_ref[:, rows] if chained else None
        for left, (part, pair, *_) in zip(lefts, terms):
            found = lax.dot_general(
                left, counts_refs[part][pair, rows, :], (((1,), (1,)), ((), ())),
                preferred_element_type=jnp.float32,
            )
            total = found if total is None else total + found
        grad_ref[:, rows] = total
        if last:
            square_ref[:, rows] = jnp.sum(total * total, axis=0, keepdims=True)

    for part in range(parts):
        mine = [term for term in terms if term[0] == part]
        if not mine:
            continue

        @pl.when(jnp.max(flag_refs[part][...]) >= EXACT)
        def _(part=part, mine=mine):
            for _, pair, *homes in mine:
                for member, (piece, place) in enumerate(homes):
                    copy = pltpu.make_async_copy(low_refs[part].at[2 * pair + member], spill_ref, sem)
                    copy.start()
                    copy.wait()
                    for start in range(0, row_local, block):
                        rows = slice(start, start + block)
                        grad_ref[:, rows] += lax.dot_general(
                            grads[piece][place], spill_ref[rows, :], (((1,), (1,)), ((), ())),
                            preferred_element_type=jnp.float32,
                        )
            if last:
                for start in range(0, row_local, block):
                    rows = slice(start, start + block)
                    final = grad_ref[:, rows]
                    square_ref[:, rows] = jnp.sum(final * final, axis=0, keepdims=True)


def grad_call(terms, flags, counts, lows, grads, before, last, pool=None, extra=()):
    parts = len(counts)
    row_local = counts[0].shape[1]
    dim_local = grads[0].shape[1]
    chained = before is not None
    vmem = pl.BlockSpec(memory_space=pltpu.VMEM)
    hbm = pl.BlockSpec(memory_space=pltpu.HBM)
    out = [jax.ShapeDtypeStruct((dim_local, row_local), jnp.float32)]
    if last:
        out.append(jax.ShapeDtypeStruct((1, row_local), jnp.float32))
    if pool is not None:
        late = 2 * (counts[1].shape[0] - pool)
        out.append(jax.ShapeDtypeStruct((late, dim_local, LANES), jnp.float32))
    return pl.pallas_call(
        functools.partial(
            grad_kernel, terms=terms, pool=pool, parts=parts, pieces=len(grads),
            block=math.gcd(row_local, 512), chained=chained, last=last,
        ),
        in_specs=[vmem] * parts + [vmem] * parts + [hbm] * parts + [vmem] * (len(grads) + chained + len(extra)),
        out_specs=[vmem] * len(out),
        out_shape=out,
        scratch_shapes=[pltpu.VMEM((row_local, LANES), jnp.bfloat16), pltpu.SemaphoreType.DMA],
        compiler_params=pltpu.CompilerParams(vmem_limit_bytes=VMEM_LIMIT),
        name="grads",
    )(*flags, *counts, *lows, *grads, *([before] if chained else []), *extra)


def crossed(mask):
    return (mask & ~3) | ((mask & 1) << 1) | ((mask & 2) >> 1)


def flip(value, mask):
    rows, dims = lax.axis_size("rows"), lax.axis_size("dims")
    pairs = [
        (row * dims + dim, (row ^ (crossed(mask) if dim % 2 else mask)) * dims + dim)
        for row in range(rows)
        for dim in range(dims)
    ]
    return lax.ppermute(value, ("rows", "dims"), pairs)


def flip_dims(value, mask):
    pairs = [(index, index ^ mask) for index in range(lax.axis_size("dims"))]
    return lax.ppermute(value, "dims", pairs)


def plan(peers):
    bits = [1 << place for place in range(peers.bit_length() - 1)]
    gather_bits = bits[-1:] + bits[:-1]
    stages = len(bits)
    blocks = [None] * stages
    phases = [None] * stages
    blocks[-1] = [0]
    for stage in reversed(range(stages)):
        if stage < stages - 1:
            blocks[stage] = phases[stage + 1] + blocks[stage + 1]
        phases[stage] = [bits[stage] ^ mask for mask in blocks[stage]]
    return bits, gather_bits, blocks, phases


def staged(table, grad_pooled, sample, row, weight, send_count):
    bits, gather_bits, blocks, phases = plan(lax.axis_size("rows"))
    stages = len(bits)
    passes = [phases[0], blocks[0]]
    peers = lax.axis_size("rows")
    now = len(phases[1]) // 2 if stages > 2 else len(passes[1]) // 2

    pieces = [grad_pooled[None]]
    homes = [(0, (0, 0))]

    def gathered():
        sizes = [sum(home[0] == index for _, home in homes) for index in range(len(pieces))]
        return [piece[:size] for piece, size in zip(pieces, sizes)]

    def arrived(piece, bit):
        homes.extend(
            [(mask ^ bit, (len(pieces), place)) for place, (mask, _) in enumerate(homes)]
        )
        pieces.append(piece)

    arrived(flip(pieces[0], gather_bits[0]), gather_bits[0])
    counts0, halves, low0, flag0, *held = count_call(
        passes[0], len(passes[0]) // 2, (send_count[None], row, sample, weight, table), pieces[0], peers
    )
    pieces[0] = held.pop()
    halves, pieces[1] = lax.optimization_barrier((halves, pieces[1]))
    sent = len(homes)
    message = flip(jnp.concatenate(gathered() + [halves]), bits[0])
    arrived(message, gather_bits[1])
    known = {mask for mask, _ in homes}
    counts1, partial1, low1, flag1 = count_call(passes[1], now, tuple(held), None, peers)
    partial1, message = lax.optimization_barrier((partial1, message))
    pieces[-1] = message
    half = len(passes[0])
    add = message[sent : sent + half].astype(jnp.float32) + message[sent + half :].astype(jnp.float32)
    held_back = 2 * now
    total = (partial1 + add)[:held_back]

    flags, counts, lows = [flag0, flag1], [counts0, counts1], [low0, low1]
    row_grad = None
    for stage in range(1, stages):
        take = len(phases[stage])
        if stage + 1 < stages:
            arrived(
                flip(jnp.concatenate(gathered()), gather_bits[stage + 1]),
                gather_bits[stage + 1],
            )
        incoming = flip(total[:take], bits[stage])
        total = total[take:]
        if stage == 1:
            spots = dict(homes)
            early, late = [], []
            for part, masks in enumerate(passes):
                for pair in range(len(masks) // 2):
                    two = masks[2 * pair : 2 * pair + 2]
                    (early if set(two) <= known else late).append((part, pair, two))
            if held_back < len(passes[1]):
                terms = [(part, pair, *(spots[mask] for mask in two)) for part, pair, two in early]
                used = 1 + max(home[0] for term in terms for home in term[2:])
                row_grad, rest = grad_call(
                    terms, flags, counts, lows, pieces[:used], None, False,
                    now, (held[4], partial1),
                )
                total = rest + add[held_back:]
            else:
                late = early + late
        if stage < stages - 1:
            total = total + incoming

    spots = dict(homes)
    terms = [(part, pair, *(spots[mask] for mask in two)) for part, pair, two in late]
    row_grad, square = grad_call(terms, flags, counts, lows, pieces, row_grad, True)
    return (total, incoming), row_grad, square


def share(square):
    terms = [square]
    mask = lax.axis_size("dims") // 2
    while mask >= 1:
        terms = terms + [flip_dims(term, mask) for term in terms]
        mask //= 2
    return terms


def update_kernel(*refs, count, block):
    terms = refs[:count]
    accum_ref, table_ref, grad_ref, own_ref, other_ref = refs[count : count + 5]
    pooled_hbm, table_hbm, accum_hbm, pooled_ref, new_ref, total_ref, sems = refs[count + 5 :]
    copies = [pltpu.make_async_copy(pooled_ref, pooled_hbm, sems.at[0])]
    pooled_ref[...] = own_ref[...] + other_ref[...]
    copies[0].start()
    row_local = grad_ref.shape[1]
    for index, start in enumerate(range(0, row_local, block)):
        rows = slice(start, start + block)
        sums = [term[:, rows] for term in terms]
        while len(sums) > 1:
            half = len(sums) // 2
            sums = [sums[place] + sums[place + half] for place in range(half)]
        squares = sums[0]
        total = accum_ref[:, rows] + squares / D
        total_ref[:, rows] = total
        scale = step_size / jnp.sqrt(total)
        new_ref[:, rows] = (
            table_ref[:, rows].astype(jnp.float32) - grad_ref[:, rows] * scale
        ).astype(jnp.bfloat16)
        copies.append(
            pltpu.make_async_copy(
                new_ref.at[:, pl.ds(start, block)], table_hbm.at[:, pl.ds(start, block)],
                sems.at[1 + index],
            )
        )
        copies[-1].start()
    copies.append(pltpu.make_async_copy(total_ref, accum_hbm, sems.at[len(copies)]))
    copies[-1].start()
    for copy in copies:
        copy.wait()


def update(table, accum, row_grad, square, sums):
    terms = share(square)
    row_local = table.shape[1]
    block = math.gcd(row_local, 1024)
    hbm = pl.BlockSpec(memory_space=pltpu.HBM)
    vmem = pl.BlockSpec(memory_space=pltpu.VMEM)
    pooled, new_table, new_accum = pl.pallas_call(
        functools.partial(update_kernel, count=len(terms), block=block),
        in_specs=[vmem] * (len(terms) + 5),
        out_specs=[hbm] * 3,
        out_shape=[
            jax.ShapeDtypeStruct(sums[0].shape, jnp.float32),
            jax.ShapeDtypeStruct(table.shape, table.dtype),
            jax.ShapeDtypeStruct((1, row_local), jnp.float32),
        ],
        scratch_shapes=[
            pltpu.VMEM(sums[0].shape, jnp.float32),
            pltpu.VMEM(table.shape, table.dtype),
            pltpu.VMEM((1, row_local), jnp.float32),
            pltpu.SemaphoreType.DMA((row_local // block + 2,)),
        ],
        compiler_params=pltpu.CompilerParams(vmem_limit_bytes=VMEM_LIMIT),
        name="update",
    )(*terms, accum[None], table, row_grad, *sums)
    return pooled[0], new_table, new_accum[0]


def fits(table, grad_pooled, peers):
    return (
        peers & (peers - 1) == 0
        and peers > 2
        and lax.axis_size("dims") & (lax.axis_size("dims") - 1) == 0
        and grad_pooled.shape[2] == LANES
        and peers * table.shape[2] * LANES * 2 <= FAST_BYTES
    )


def shards(table, accum, grad_pooled, sample_slot, row_slot, weight, send_count):
    peers = lax.axis_size("rows")
    if not fits(table, grad_pooled, peers):
        return plain(table, accum, grad_pooled, sample_slot, row_slot, weight, send_count)
    outs = []
    for feature in range(table.shape[0]):
        sums, row_grad, square = staged(
            table[feature], grad_pooled[feature], sample_slot[feature, 0],
            row_slot[feature, 0], weight[feature, 0], send_count[feature, 0],
        )
        outs.append(update(table[feature], accum[feature], row_grad, square, sums))
    return tuple(jnp.stack(out) for out in zip(*outs))


def plain(table, accum, grad_pooled, sample_slot, row_slot, weight, send_count):
    feat_count, dim_local, row_local = table.shape
    peer_count = lax.axis_size("rows")
    own_samples = grad_pooled.shape[2]
    slot_count = sample_slot.shape[3]
    entry_count = peer_count * slot_count
    block_rows = math.gcd(row_local, 512)
    block_count = row_local // block_rows
    sample_local = sample_slot.reshape(feat_count, peer_count, slot_count)
    row_index = row_slot.reshape(feat_count, peer_count, slot_count)
    flat_rows = row_index.reshape(feat_count, 1, entry_count)
    live_count = send_count.reshape(feat_count, peer_count)
    slot_iota = lax.broadcasted_iota(jnp.int32, (1, 1, slot_count), 2)
    live_mask = slot_iota < live_count[:, :, None]
    weights = jnp.where(live_mask, weight.reshape(feat_count, peer_count, slot_count), 0)
    flat_weights = weights.reshape(feat_count, 1, entry_count).astype(jnp.bfloat16)
    block_iota = lax.broadcasted_iota(jnp.int32, (1, block_rows, 1), 1)

    def lookup_block(carry, block):
        start = block * block_rows
        table_part = lax.dynamic_slice_in_dim(table, start, block_rows, 2)
        selector = (flat_rows == block_iota + start).astype(jnp.bfloat16)
        return (
            carry
            + jnp.einsum("fdr,fre->fde", table_part, selector, preferred_element_type=jnp.float32),
            None,
        )

    looked_up, _ = lax.scan(
        lookup_block,
        jnp.zeros((feat_count, dim_local, entry_count), jnp.float32),
        jnp.arange(block_count, dtype=jnp.int32),
    )
    picked = looked_up.astype(jnp.bfloat16).reshape(feat_count, dim_local, peer_count, slot_count)
    positions = lax.broadcasted_iota(jnp.int32, (1, 1, 1, own_samples), 3)
    onehot = jnp.where(sample_local[..., None] == positions, weights[..., None], 0).astype(
        jnp.bfloat16
    )
    pooled = lax.psum_scatter(
        jnp.einsum("fdnk,fnkj->nfdj", picked, onehot, preferred_element_type=jnp.float32),
        "rows",
        scatter_dimension=0,
        tiled=True,
    ).reshape(feat_count, dim_local, own_samples)
    all_grads = lax.all_gather(grad_pooled, "rows", axis=2, tiled=True)
    all_grads = all_grads.reshape(feat_count, dim_local, peer_count, own_samples)
    selector = (sample_local[..., None] == positions).astype(jnp.bfloat16)
    entry_values = jnp.einsum(
        "fdnj,fnkj->fdnk", all_grads, selector, preferred_element_type=jnp.float32
    ).astype(jnp.bfloat16)
    entry_flat = entry_values.reshape(feat_count, dim_local, entry_count)

    def gradient_block(block):
        start = block * block_rows
        weighted = jnp.where(flat_rows == block_iota + start, flat_weights, 0)
        return jnp.einsum("fde,fre->fdr", entry_flat, weighted, preferred_element_type=jnp.float32)

    grad_blocks = lax.map(gradient_block, jnp.arange(block_count, dtype=jnp.int32))
    row_grad = jnp.moveaxis(grad_blocks, 0, 2).reshape(feat_count, dim_local, row_local)
    squares = jnp.sum(row_grad * row_grad, axis=1)
    norm_total = lax.psum(squares, "dims")
    new_accum = accum + norm_total / D
    new_table = (
        table.astype(jnp.float32) - step_size * row_grad / jnp.sqrt(new_accum)[:, None, :]
    ).astype(jnp.bfloat16)
    return (pooled, new_table, new_accum)


def solution(mesh):
    return jax.shard_map(
        shards,
        mesh=mesh,
        in_specs=(
            P(None, "dims", "rows"),
            P(None, "rows"),
            P(None, "dims", "rows"),
            P(None, "rows", None, None),
            P(None, "rows", None, None),
            P(None, "rows", None, None),
            P(None, "rows", None),
        ),
        out_specs=(P(None, "dims", "rows"), P(None, "dims", "rows"), P(None, "rows")),
        check_vma=False,
    )
```
